256 devices in a mesh: roll: 4 (over z_lo, core), mach: 16 (over y, x), cross: 4 (over z_hi).
Axes of the slice: x: 4, y: 4, z: 8 (z_hi: 4, z_lo: 2; z = z_hi * 2 + z_lo), core: 2. Of those that a mesh axis runs over, the one named last changes fastest.
Arguments:
- density: bfloat16 [128, 4096, 2048], P('roll', 'mach', 'cross'), may hold values from 0 to 1
- roll_start: float32 [32, 128], P(None, 'roll'), may hold values from 0.05 to 1
- mach_factor: bfloat16 [32, 4096], P(None, 'mach'), may hold values from 0.0099487305 to 1
- cross_factor: bfloat16 [32, 2048], P(None, 'cross'), may hold values from 0.0099487305 to 1
Outputs:
- roll_factor: float32 [32, 128], P(None, 'roll')
- mode_two: float32 [32, 4096], P(None, ('mach', 'cross'))
The draws below stay inside these ranges and needn't reach their ends.
All inputs are finite; a program needn't handle non-finite values.
Results may differ from the reference program's by a relative error of at most 0.0003.
Values sent between devices are 32-bit elements; how exact they have to be, the bound alone decides.
A program may use at most 64 MiB of HBM per device.

```python
import math
import jax
import jax.numpy as jnp
from jax import lax

R = 32
J = 4096
K = 2048
ROLLS = 128


def lognormal_vector(key, count):
    return jnp.exp(jax.random.normal(key, (count,), jnp.float32))


def draw_density(key, part):
    roll_one = lognormal_vector(jax.random.fold_in(key, 11), ROLLS)[:, None, None]
    mach_one = lognormal_vector(jax.random.fold_in(key, 12), J)[None, :, None]
    cross_one = lognormal_vector(jax.random.fold_in(key, 13), K)[None, None, :]
    roll_two = lognormal_vector(jax.random.fold_in(key, 21), ROLLS)[:, None, None]
    mach_two = lognormal_vector(jax.random.fold_in(key, 22), J)[None, :, None]
    cross_two = lognormal_vector(jax.random.fold_in(key, 23), K)[None, None, :]
    noise_key = jax.random.fold_in(key, 31)
    noise = jnp.exp(0.8 * jax.random.normal(noise_key, (ROLLS, J, K), jnp.float32))
    base = roll_one * mach_one * cross_one + roll_two * mach_two * cross_two
    level = 0.25 * base * noise
    return (level / (1.0 + level)).astype(jnp.bfloat16)


def steps_of(stream_key, shape, pieces, smallest, largest):
    level, own = 1.0, jax.random.fold_in(stream_key, 6)
    for position, shards_of in pieces:
        steps = jnp.exp(jax.random.uniform(jax.random.fold_in(own, position), (shards_of,), jnp.float32, smallest / len(pieces), largest / len(pieces)))
        level = level * jnp.repeat(steps, shape[position] // shards_of).reshape([-1 if axis == position else 1 for axis in range(len(shape))])
    return level


def setup_inputs(seed: int = 0) -> dict:
    keys = jax.random.split(jax.random.key(seed), 5)
    density = draw_density(jax.random.fold_in(keys[4], 71), 0)
    roll_start = jnp.clip(jnp.exp(math.log(1.0) - 2.9957323 * jax.random.uniform(keys[1], (R, ROLLS), jnp.float32) ** steps_of(keys[1], (R, ROLLS), ((1, 4),), -0.2, 0.2)), 0.05, 1.0)
    mach_factor = jnp.clip(jnp.exp(math.log(1.0) - 4.61031033 * jax.random.uniform(keys[2], (R, J), jnp.float32) ** steps_of(keys[2], (R, J), ((1, 16),), -0.2, 0.2)), 0.0099487305, 1.0).astype(jnp.bfloat16)
    cross_factor = jnp.clip(jnp.exp(math.log(1.0) - 4.61031033 * jax.random.uniform(keys[3], (R, K), jnp.float32) ** steps_of(keys[3], (R, K), ((1, 4),), -0.2, 0.2)), 0.0099487305, 1.0).astype(jnp.bfloat16)
    return {"density": density, "roll_start": roll_start, "mach_factor": mach_factor, "cross_factor": cross_factor}


def hals_rows(roll_rows, mttkrp, gram):
    def column_step(column, rows):
        column = jnp.asarray(column).astype(jnp.int32)
        gram_row = lax.dynamic_slice_in_dim(gram, column, 1, 0)
        diag_entry = lax.dynamic_slice_in_dim(gram_row, column, 1, 1)
        current = lax.dynamic_slice_in_dim(rows, column, 1, 0)
        target = lax.dynamic_slice_in_dim(mttkrp, column, 1, 0)
        mixed = jnp.dot(gram_row, rows, precision=lax.Precision.HIGHEST)
        updated = jnp.maximum(current + (target - mixed) / diag_entry, 0.0)
        return lax.dynamic_update_slice_in_dim(rows, updated, column, 0)
    return lax.fori_loop(0, roll_rows.shape[0], column_step, roll_rows)


def reference(density, roll_start, mach_factor, cross_factor):
    def one_roll(slab):
        return lax.dot_general(cross_factor, slab, (((1,), (1,)), ((), ())), preferred_element_type=jnp.float32)
    partial_value = lax.map(one_roll, density)
    mttkrp = jnp.einsum('irj,rj->ri', partial_value, mach_factor.astype(jnp.float32), precision=lax.Precision.HIGHEST)
    gram_mach = jnp.dot(mach_factor, mach_factor.T, preferred_element_type=jnp.float32)
    gram_cross = jnp.dot(cross_factor, cross_factor.T, preferred_element_type=jnp.float32)
    gram = gram_mach * gram_cross
    roll_factor = hals_rows(roll_start, mttkrp, gram)
    total = jnp.einsum('irj,ri->rj', partial_value, roll_factor, precision=lax.Precision.HIGHEST)
    scale = R / (ROLLS * K)
    mode_two = total * scale
    return roll_factor, mode_two
```

```python
import jax
import jax.numpy as jnp
from jax import lax
from jax.sharding import PartitionSpec as P


def hals_rows(roll_rows, mttkrp, gram):
    def column_step(column, rows):
        column = jnp.asarray(column).astype(jnp.int32)
        gram_row = lax.dynamic_slice_in_dim(gram, column, 1, 0)
        diag_entry = lax.dynamic_slice_in_dim(gram_row, column, 1, 1)
        current = lax.dynamic_slice_in_dim(rows, column, 1, 0)
        target = lax.dynamic_slice_in_dim(mttkrp, column, 1, 0)
        mixed = jnp.dot(gram_row, rows, precision=lax.Precision.HIGHEST)
        updated = jnp.maximum(current + (target - mixed) / diag_entry, 0.0)
        return lax.dynamic_update_slice_in_dim(rows, updated, column, 0)
    return lax.fori_loop(0, roll_rows.shape[0], column_step, roll_rows)


def local(density, roll_start, mach_factor, cross_factor):
    rolls_here, bins_here, cross_here = density.shape
    rank = cross_factor.shape[0]
    flat = density.reshape(rolls_here * bins_here, cross_here)
    partial_value = lax.dot_general(cross_factor, flat, (((1,), (1,)), ((), ())), preferred_element_type=jnp.float32)
    partial_value = partial_value.reshape(rank, rolls_here, bins_here)
    local_terms = jnp.einsum("rij,rj->ri", partial_value, mach_factor.astype(jnp.float32), precision=lax.Precision.HIGHEST)
    local_mach = jnp.dot(mach_factor, mach_factor.T, preferred_element_type=jnp.float32)
    local_cross = jnp.dot(cross_factor, cross_factor.T, preferred_element_type=jnp.float32)
    a = lax.axis_index("roll"); m = lax.axis_index("mach"); c = lax.axis_index("cross")
    nroll = lax.axis_size("roll")
    slots = jnp.zeros((nroll + 2, rank, rank), jnp.float32)
    slots = lax.dynamic_update_slice_in_dim(slots, local_terms[None], a, 0)
    slots = slots.at[nroll].set(jnp.where((a == 0) & (c == 0), local_mach, 0.0))
    slots = slots.at[nroll + 1].set(jnp.where((a == 0) & (m == 0), local_cross, 0.0))
    tot = lax.psum(slots, ("roll", "mach", "cross"))
    mttkrp = lax.dynamic_index_in_dim(tot, a, 0, keepdims=False)
    gram = tot[nroll] * tot[nroll + 1]
    roll_factor = hals_rows(roll_start, mttkrp, gram)
    term = jnp.einsum("rij,ri->rj", partial_value, roll_factor, precision=lax.Precision.HIGHEST)
    nm = lax.axis_size("mach")
    ms = jnp.zeros((nm,) + term.shape, jnp.float32)
    ms = lax.dynamic_update_slice_in_dim(ms, term[None], m, 0)
    whole = lax.psum(ms, ("roll", "mach", "cross"))
    whole = lax.dynamic_index_in_dim(whole, m, 0, keepdims=False)
    span = whole.shape[1] // lax.axis_size("cross")
    total = lax.dynamic_slice_in_dim(whole, c * span, span, 1)
    scale = rank / (rolls_here * nroll * cross_here * lax.axis_size("cross"))
    return (roll_factor, total * scale)


def solution(mesh):
    in_specs = (P("roll", "mach", "cross"), P(None, "roll"), P(None, "mach"), P(None, "cross"))
    out_specs = (P(None, "roll"), P(None, ("mach", "cross")))
    return jax.shard_map(local, mesh=mesh, in_specs=in_specs, out_specs=out_specs, check_vma=False)
```

```python
import functools

import jax
import jax.numpy as jnp
from jax import lax
from jax.experimental import pallas as pl
from jax.experimental.pallas import tpu as pltpu
from jax.sharding import PartitionSpec as P

MESH = pl.DeviceIdType.MESH
VMEM = pltpu.VMEM


def gram_sum_kernel(n_cross, pay_ref, out_ref, recv, send_sem, recv_sem):
    roll = lax.axis_index("roll")
    mach = lax.axis_index("mach")
    cross = lax.axis_index("cross")
    group = recv.shape[0]
    n_mach = group // n_cross
    me = mach * n_cross + cross

    barrier = pltpu.get_barrier_semaphore()

    def greet(p, carry):
        @pl.when(p != me)
        def _():
            pl.semaphore_signal(barrier, inc=1, device_id=(roll, p // n_cross, p % n_cross), device_id_type=MESH)
        return carry

    lax.fori_loop(0, group, greet, 0)
    pl.semaphore_wait(barrier, group - 1)

    def each_peer(p, action):
        pm = p // n_cross
        pc = p % n_cross
        same_cross = jnp.logical_and(pc == cross, pm != mach)
        same_mach = jnp.logical_and(pm == mach, pc != cross)
        other = jnp.logical_and(pm != mach, pc != cross)

        @pl.when(same_cross)
        def _():
            action(p, 0, 16)

        @pl.when(same_mach)
        def _():
            action(p, 8, 16)

        @pl.when(other)
        def _():
            action(p, 8, 8)

    def start(p, lo, size):
        pltpu.make_async_remote_copy(
            src_ref=pay_ref.at[pl.ds(lo, size)],
            dst_ref=recv.at[me, pl.ds(lo, size)],
            send_sem=send_sem.at[p],
            recv_sem=recv_sem.at[me],
            device_id=(roll, p // n_cross, p % n_cross),
            device_id_type=MESH,
        ).start()

    def finish(p, lo, size):
        pltpu.make_async_remote_copy(
            src_ref=pay_ref.at[pl.ds(lo, size)],
            dst_ref=recv.at[p, pl.ds(lo, size)],
            send_sem=send_sem.at[p],
            recv_sem=recv_sem.at[p],
            device_id=(roll, p // n_cross, p % n_cross),
            device_id_type=MESH,
        ).wait()

    def send_loop(p, carry):
        each_peer(p, start)
        return carry

    def wait_loop(p, carry):
        each_peer(p, finish)
        return carry

    lax.fori_loop(0, group, send_loop, 0)
    recv[me] = pay_ref[...]
    lax.fori_loop(0, group, wait_loop, 0)

    terms = recv[0, 8:16, :]
    for p in range(1, group):
        terms = terms + recv[p, 8:16, :]
    gm = recv[cross, 0:8, :]
    for q in range(1, n_mach):
        gm = gm + recv[q * n_cross + cross, 0:8, :]
    gc = recv[mach * n_cross, 16:24, :]
    for q in range(1, n_cross):
        gc = gc + recv[mach * n_cross + q, 16:24, :]
    out_ref[0:8, :] = gm
    out_ref[8:16, :] = terms
    out_ref[16:24, :] = gc


def mode_sum_kernel(n_cross, scale, pieces_ref, out_ref, recv, send_sem, recv_sem):
    roll = lax.axis_index("roll")
    mach = lax.axis_index("mach")
    cross = lax.axis_index("cross")
    group = recv.shape[0]
    me = roll * n_cross + cross

    barrier = pltpu.get_barrier_semaphore()

    def greet(p, carry):
        @pl.when(p != me)
        def _():
            pl.semaphore_signal(barrier, inc=1, device_id=(p // n_cross, mach, p % n_cross), device_id_type=MESH)
        return carry

    lax.fori_loop(0, group, greet, 0)
    pl.semaphore_wait(barrier, group - 1)

    def send_loop(p, carry):
        @pl.when(p != me)
        def _():
            pltpu.make_async_remote_copy(
                src_ref=pieces_ref.at[p % n_cross],
                dst_ref=recv.at[me],
                send_sem=send_sem.at[p],
                recv_sem=recv_sem.at[me],
                device_id=(p // n_cross, mach, p % n_cross),
                device_id_type=MESH,
            ).start()
        return carry

    def wait_loop(p, carry):
        @pl.when(p != me)
        def _():
            pltpu.make_async_remote_copy(
                src_ref=pieces_ref.at[p % n_cross],
                dst_ref=recv.at[p],
                send_sem=send_sem.at[p],
                recv_sem=recv_sem.at[p],
                device_id=(p // n_cross, mach, p % n_cross),
                device_id_type=MESH,
            ).wait()
        return carry

    lax.fori_loop(0, group, send_loop, 0)
    recv[me] = pieces_ref[cross]
    lax.fori_loop(0, group, wait_loop, 0)

    total = recv[0]
    for p in range(1, group):
        total = total + recv[p]
    out_ref[...] = total * scale


def hals_kernel(sums_ref, start_ref, out_ref):
    gram = sums_ref[0] * sums_ref[2]
    target = sums_ref[1]
    out_ref[...] = start_ref[...]
    for r in range(out_ref.shape[0]):
        rows = out_ref[...]
        mixed = jnp.sum(gram[:, r : r + 1] * rows, axis=0, keepdims=True)
        current = rows[r : r + 1, :]
        updated = jnp.maximum(current + (target[r : r + 1, :] - mixed) / gram[r : r + 1, r : r + 1], 0.0)
        out_ref[r : r + 1, :] = updated


def local(density, roll_start, mach_factor, cross_factor):
    rolls_here, bins_here, cross_here = density.shape
    rank = cross_factor.shape[0]
    n_roll = lax.axis_size("roll")
    n_mach = lax.axis_size("mach")
    n_cross = lax.axis_size("cross")
    flat = density.reshape(rolls_here * bins_here, cross_here)
    partial_value = lax.dot_general(
        cross_factor, flat, (((1,), (1,)), ((), ())), preferred_element_type=jnp.float32
    )
    partial_value = partial_value.reshape(rank, rolls_here, bins_here)
    local_terms = jnp.einsum(
        "rij,rj->ri", partial_value, mach_factor.astype(jnp.float32), precision=lax.Precision.HIGHEST
    )
    local_mach = jnp.dot(mach_factor, mach_factor.T, preferred_element_type=jnp.float32)
    local_cross = jnp.dot(cross_factor, cross_factor.T, preferred_element_type=jnp.float32)
    pay = jnp.stack([local_mach, local_terms, local_cross]).reshape(24, 128)

    sums = pl.pallas_call(
        functools.partial(gram_sum_kernel, n_cross),
        out_shape=jax.ShapeDtypeStruct((24, 128), jnp.float32),
        in_specs=[pl.BlockSpec(memory_space=VMEM)],
        out_specs=pl.BlockSpec(memory_space=VMEM),
        scratch_shapes=[
            VMEM((n_mach * n_cross, 24, 128), jnp.float32),
            pltpu.SemaphoreType.DMA((n_mach * n_cross,)),
            pltpu.SemaphoreType.DMA((n_mach * n_cross,)),
        ],
        compiler_params=pltpu.CompilerParams(collective_id=0, has_side_effects=True),
    )(pay)
    sums = sums.reshape(3, rank, rank)

    roll_factor = pl.pallas_call(
        hals_kernel,
        out_shape=jax.ShapeDtypeStruct(roll_start.shape, jnp.float32),
        in_specs=[pl.BlockSpec(memory_space=VMEM)] * 2,
        out_specs=pl.BlockSpec(memory_space=VMEM),
    )(sums, roll_start)

    term = jnp.einsum("rij,ri->rj", partial_value, roll_factor, precision=lax.Precision.HIGHEST)
    span = bins_here // n_cross
    pieces = term.reshape(rank, n_cross, span).transpose(1, 0, 2).reshape(n_cross, rank * span // 128, 128)
    scale = rank / (rolls_here * n_roll * cross_here * n_cross)
    mode = pl.pallas_call(
        functools.partial(mode_sum_kernel, n_cross, scale),
        out_shape=jax.ShapeDtypeStruct(pieces.shape[1:], jnp.float32),
        in_specs=[pl.BlockSpec(memory_space=VMEM)],
        out_specs=pl.BlockSpec(memory_space=VMEM),
        scratch_shapes=[
            VMEM((n_roll * n_cross,) + pieces.shape[1:], jnp.float32),
            pltpu.SemaphoreType.DMA((n_roll * n_cross,)),
            pltpu.SemaphoreType.DMA((n_roll * n_cross,)),
        ],
        compiler_params=pltpu.CompilerParams(collective_id=1, has_side_effects=True),
    )(pieces)
    mode_two = mode.reshape(rank, span)
    return (roll_factor, mode_two)


def solution(mesh):
    in_specs = (P("roll", "mach", "cross"), P(None, "roll"), P(None, "mach"), P(None, "cross"))
    out_specs = (P(None, "roll"), P(None, ("mach", "cross")))
    return jax.shard_map(local, mesh=mesh, in_specs=in_specs, out_specs=out_specs, check_vma=False)
```

```python
import functools

import jax
import jax.numpy as jnp
from jax import lax
from jax.experimental import pallas as pl
from jax.experimental.pallas import tpu as pltpu
from jax.sharding import PartitionSpec as P

MESH = pl.DeviceIdType.MESH
VMEM = pltpu.VMEM


def fused_kernel(n_roll, n_cross, scale, pay_ref, part_ref, start_ref, rf_ref, mode_ref,
                 recv_a, send_a, got_a, gm_s, mt_s, gc_s, term_s, pieces, recv_b, send_b, got_b, total_s):
    roll = lax.axis_index("roll")
    mach = lax.axis_index("mach")
    cross = lax.axis_index("cross")
    group_a = recv_a.shape[0]
    group_b = recv_b.shape[0]
    n_mach = group_a // n_cross
    me_a = mach * n_cross + cross
    me_b = roll * n_cross + cross
    rank = rf_ref.shape[0]

    def peer_a(p):
        return (roll, p // n_cross, p % n_cross)

    def peer_b(p):
        return (p // n_cross, mach, p % n_cross)

    barrier = pltpu.get_barrier_semaphore()

    def greet_a(p, carry):
        @pl.when(p != me_a)
        def _():
            pl.semaphore_signal(barrier, inc=1, device_id=peer_a(p), device_id_type=MESH)
        return carry

    def greet_b(p, carry):
        @pl.when(p // n_cross != roll)
        def _():
            pl.semaphore_signal(barrier, inc=1, device_id=peer_b(p), device_id_type=MESH)
        return carry

    lax.fori_loop(0, group_a, greet_a, 0)
    lax.fori_loop(0, group_b, greet_b, 0)
    pl.semaphore_wait(barrier, group_a - 1 + group_b - n_cross)

    def each_peer(p, action):
        pm = p // n_cross
        pc = p % n_cross

        @pl.when(jnp.logical_and(pc == cross, pm != mach))
        def _():
            action(p, 0, 16)

        @pl.when(jnp.logical_and(pm == mach, pc != cross))
        def _():
            action(p, 8, 16)

        @pl.when(jnp.logical_and(pm != mach, pc != cross))
        def _():
            action(p, 8, 8)

    def start_a(p, lo, size):
        pltpu.make_async_remote_copy(
            src_ref=pay_ref.at[pl.ds(lo, size)], dst_ref=recv_a.at[me_a, pl.ds(lo, size)],
            send_sem=send_a.at[p], recv_sem=got_a.at[me_a], device_id=peer_a(p), device_id_type=MESH,
        ).start()

    def finish_a(p, lo, size):
        pltpu.make_async_remote_copy(
            src_ref=pay_ref.at[pl.ds(lo, size)], dst_ref=recv_a.at[p, pl.ds(lo, size)],
            send_sem=send_a.at[p], recv_sem=got_a.at[p], device_id=peer_a(p), device_id_type=MESH,
        ).wait()

    def send_loop_a(p, carry):
        each_peer(p, start_a)
        return carry

    def wait_loop_a(p, carry):
        each_peer(p, finish_a)
        return carry

    lax.fori_loop(0, group_a, send_loop_a, 0)
    recv_a[me_a] = pay_ref[...]
    lax.fori_loop(0, group_a, wait_loop_a, 0)

    terms = recv_a[0, 8:16, :]
    for p in range(1, group_a):
        terms = terms + recv_a[p, 8:16, :]
    gm = recv_a[cross, 0:8, :]
    for q in range(1, n_mach):
        gm = gm + recv_a[q * n_cross + cross, 0:8, :]
    gc = recv_a[mach * n_cross, 16:24, :]
    for q in range(1, n_cross):
        gc = gc + recv_a[mach * n_cross + q, 16:24, :]
    for g in range(4):
        lanes = slice(g * 32, (g + 1) * 32)
        gm_s[pl.ds(g, 8, stride=4), :] = gm[:, lanes]
        mt_s[pl.ds(g, 8, stride=4), :] = terms[:, lanes]
        gc_s[pl.ds(g, 8, stride=4), :] = gc[:, lanes]

    gram = gm_s[...] * gc_s[...]
    target = mt_s[...]
    rf_ref[...] = start_ref[...]
    for r in range(rank):
        rows = rf_ref[...]
        mixed = jnp.sum(gram[:, r : r + 1] * rows, axis=0, keepdims=True)
        current = rows[r : r + 1, :]
        updated = jnp.maximum(current + (target[r : r + 1, :] - mixed) / gram[r : r + 1, r : r + 1], 0.0)
        rf_ref[r : r + 1, :] = updated

    factor = rf_ref[...]
    term = part_ref[0] * factor[:, 0:1]
    for i in range(1, part_ref.shape[0]):
        term = term + part_ref[i] * factor[:, i : i + 1]
    term_s[...] = term
    span = term_s.shape[1] // n_cross
    per_row = 128 // span
    for c in range(n_cross):
        for r in range(rank):
            pieces[c, r // per_row : r // per_row + 1, (r % per_row) * span : (r % per_row + 1) * span] = (
                term_s[r : r + 1, c * span : (c + 1) * span])

    def send_loop_b(p, carry):
        @pl.when(p != me_b)
        def _():
            pltpu.make_async_remote_copy(
                src_ref=pieces.at[p % n_cross], dst_ref=recv_b.at[me_b],
                send_sem=send_b.at[p], recv_sem=got_b.at[me_b], device_id=peer_b(p), device_id_type=MESH,
            ).start()
        return carry

    def wait_loop_b(p, carry):
        @pl.when(p != me_b)
        def _():
            pltpu.make_async_remote_copy(
                src_ref=pieces.at[p % n_cross], dst_ref=recv_b.at[p],
                send_sem=send_b.at[p], recv_sem=got_b.at[p], device_id=peer_b(p), device_id_type=MESH,
            ).wait()
        return carry

    lax.fori_loop(0, group_b, send_loop_b, 0)
    recv_b[me_b] = pieces[cross]
    lax.fori_loop(0, group_b, wait_loop_b, 0)

    total = recv_b[0]
    for p in range(1, group_b):
        total = total + recv_b[p]
    total_s[...] = total * scale
    for r in range(rank):
        mode_ref[r : r + 1, :] = total_s[r // per_row : r // per_row + 1, (r % per_row) * span : (r % per_row + 1) * span]


def local(density, roll_start, mach_factor, cross_factor):
    rolls_here, bins_here, cross_here = density.shape
    rank = cross_factor.shape[0]
    n_roll = lax.axis_size("roll")
    n_mach = lax.axis_size("mach")
    n_cross = lax.axis_size("cross")
    flat = density.reshape(rolls_here * bins_here, cross_here)
    partial_value = lax.dot_general(
        cross_factor, flat, (((1,), (1,)), ((), ())), preferred_element_type=jnp.float32
    )
    partial_value = partial_value.reshape(rank, rolls_here, bins_here)
    local_terms = jnp.einsum(
        "rij,rj->ri", partial_value, mach_factor.astype(jnp.float32), precision=lax.Precision.HIGHEST
    )
    local_mach = jnp.dot(mach_factor, mach_factor.T, preferred_element_type=jnp.float32)
    local_cross = jnp.dot(cross_factor, cross_factor.T, preferred_element_type=jnp.float32)
    pay = jnp.stack([local_mach, local_terms, local_cross]).reshape(3 * rank * rank // 128, 128)

    span = bins_here // n_cross
    scale = rank / (rolls_here * n_roll * cross_here * n_cross)
    roll_factor, mode_two = pl.pallas_call(
        functools.partial(fused_kernel, n_roll, n_cross, scale),
        out_shape=(
            jax.ShapeDtypeStruct(roll_start.shape, jnp.float32),
            jax.ShapeDtypeStruct((rank, span), jnp.float32),
        ),
        in_specs=[pl.BlockSpec(memory_space=VMEM)] * 3,
        out_specs=[pl.BlockSpec(memory_space=VMEM)] * 2,
        scratch_shapes=[
            VMEM((n_mach * n_cross,) + pay.shape, jnp.float32),
            pltpu.SemaphoreType.DMA((n_mach * n_cross,)),
            pltpu.SemaphoreType.DMA((n_mach * n_cross,)),
            VMEM((rank, rank), jnp.float32),
            VMEM((rank, rank), jnp.float32),
            VMEM((rank, rank), jnp.float32),
            VMEM((rank, bins_here), jnp.float32),
            VMEM((n_cross, rank * span // 128, 128), jnp.float32),
            VMEM((n_roll * n_cross, rank * span // 128, 128), jnp.float32),
            pltpu.SemaphoreType.DMA((n_roll * n_cross,)),
            pltpu.SemaphoreType.DMA((n_roll * n_cross,)),
            VMEM((rank * span // 128, 128), jnp.float32),
        ],
        compiler_params=pltpu.CompilerParams(collective_id=0, has_side_effects=True),
    )(pay, partial_value.transpose(1, 0, 2), roll_start)
    return (roll_factor, mode_two)


def solution(mesh):
    in_specs = (P("roll", "mach", "cross"), P(None, "roll"), P(None, "mach"), P(None, "cross"))
    out_specs = (P(None, "roll"), P(None, ("mach", "cross")))
    return jax.shard_map(local, mesh=mesh, in_specs=in_specs, out_specs=out_specs, check_vma=False)
```

```python
import functools

import jax
import jax.numpy as jnp
from jax import lax
from jax.experimental import pallas as pl
from jax.experimental.pallas import tpu as pltpu
from jax.sharding import PartitionSpec as P

MESH = pl.DeviceIdType.MESH
VMEM = pltpu.VMEM


def fused_kernel(n_roll, n_cross, scale, n_chunks, dens_hbm, cross_ref, mach_ref, start_ref, rf_ref, mode_ref,
                 dens_v, dens_sem, part_ref, local_s, pay_ref,
                 recv_a, send_a, got_a, gm_s, mt_s, gc_s, term_s, pieces, recv_b, send_b, got_b, total_s):
    roll = lax.axis_index("roll")
    mach = lax.axis_index("mach")
    cross = lax.axis_index("cross")
    group_a = recv_a.shape[0]
    group_b = recv_b.shape[0]
    n_mach = group_a // n_cross
    me_a = mach * n_cross + cross
    me_b = roll * n_cross + cross
    rank = rf_ref.shape[0]

    def peer_a(p):
        return (roll, p // n_cross, p % n_cross)

    def peer_b(p):
        return (p // n_cross, mach, p % n_cross)

    rolls_here = dens_v.shape[0]
    chunk = rolls_here // n_chunks
    loads = [
        pltpu.make_async_copy(dens_hbm.at[pl.ds(k * chunk, chunk)], dens_v.at[pl.ds(k * chunk, chunk)], dens_sem.at[k])
        for k in range(n_chunks)
    ]
    for load in loads:
        load.start()

    barrier = pltpu.get_barrier_semaphore()

    def greet_a(p, carry):
        @pl.when(p != me_a)
        def _():
            pl.semaphore_signal(barrier, inc=1, device_id=peer_a(p), device_id_type=MESH)
        return carry

    def greet_b(p, carry):
        @pl.when(p // n_cross != roll)
        def _():
            pl.semaphore_signal(barrier, inc=1, device_id=peer_b(p), device_id_type=MESH)
        return carry

    lax.fori_loop(0, group_a, greet_a, 0)
    lax.fori_loop(0, group_b, greet_b, 0)

    nt = (((1,), (1,)), ((), ()))
    cross_f = cross_ref[...]
    mach_f = mach_ref[...]
    mach_w = mach_f.astype(jnp.float32)
    local_s[0] = lax.dot_general(mach_f, mach_f, nt, preferred_element_type=jnp.float32)
    local_s[2] = lax.dot_general(cross_f, cross_f, nt, preferred_element_type=jnp.float32)
    lane = lax.broadcasted_iota(jnp.int32, (rank, rolls_here), 1)
    terms_local = jnp.zeros((rank, rolls_here), jnp.float32)
    for k in range(n_chunks):
        loads[k].wait()
        for i in range(k * chunk, (k + 1) * chunk):
            value = lax.dot_general(cross_f, dens_v[i], nt, preferred_element_type=jnp.float32)
            part_ref[i] = value
            column = jnp.sum(value * mach_w, axis=1, keepdims=True)
            terms_local = jnp.where(lane == i, column, terms_local)
    local_s[1] = terms_local
    for k in range(3):
        for g in range(4):
            pay_ref[8 * k : 8 * k + 8, g * 32 : (g + 1) * 32] = local_s[k, pl.ds(g, 8, stride=4), :]

    pl.semaphore_wait(barrier, group_a - 1 + group_b - n_cross)

    def each_peer(p, action):
        pm = p // n_cross
        pc = p % n_cross

        @pl.when(jnp.logical_and(pc == cross, pm != mach))
        def _():
            action(p, 0, 16)

        @pl.when(jnp.logical_and(pm == mach, pc != cross))
        def _():
            action(p, 8, 16)

        @pl.when(jnp.logical_and(pm != mach, pc != cross))
        def _():
            action(p, 8, 8)

    def start_a(p, lo, size):
        pltpu.make_async_remote_copy(
            src_ref=pay_ref.at[pl.ds(lo, size)], dst_ref=recv_a.at[me_a, pl.ds(lo, size)],
            send_sem=send_a.at[p], recv_sem=got_a.at[me_a], device_id=peer_a(p), device_id_type=MESH,
        ).start()

    def finish_a(p, lo, size):
        pltpu.make_async_remote_copy(
            src_ref=pay_ref.at[pl.ds(lo, size)], dst_ref=recv_a.at[p, pl.ds(lo, size)],
            send_sem=send_a.at[p], recv_sem=got_a.at[p], device_id=peer_a(p), device_id_type=MESH,
        ).wait()

    def send_loop_a(p, carry):
        each_peer(p, start_a)
        return carry

    def wait_loop_a(p, carry):
        each_peer(p, finish_a)
        return carry

    lax.fori_loop(0, group_a, send_loop_a, 0)
    recv_a[me_a] = pay_ref[...]
    lax.fori_loop(0, group_a, wait_loop_a, 0)

    terms = recv_a[0, 8:16, :]
    for p in range(1, group_a):
        terms = terms + recv_a[p, 8:16, :]
    gm = recv_a[cross, 0:8, :]
    for q in range(1, n_mach):
        gm = gm + recv_a[q * n_cross + cross, 0:8, :]
    gc = recv_a[mach * n_cross, 16:24, :]
    for q in range(1, n_cross):
        gc = gc + recv_a[mach * n_cross + q, 16:24, :]
    for g in range(4):
        lanes = slice(g * 32, (g + 1) * 32)
        gm_s[pl.ds(g, 8, stride=4), :] = gm[:, lanes]
        mt_s[pl.ds(g, 8, stride=4), :] = terms[:, lanes]
        gc_s[pl.ds(g, 8, stride=4), :] = gc[:, lanes]

    gram = gm_s[...] * gc_s[...]
    target = mt_s[...]
    rf_ref[...] = start_ref[...]
    for r in range(rank):
        rows = rf_ref[...]
        mixed = jnp.sum(gram[:, r : r + 1] * rows, axis=0, keepdims=True)
        current = rows[r : r + 1, :]
        updated = jnp.maximum(current + (target[r : r + 1, :] - mixed) / gram[r : r + 1, r : r + 1], 0.0)
        rf_ref[r : r + 1, :] = updated

    factor = rf_ref[...]
    term = part_ref[0] * factor[:, 0:1]
    for i in range(1, part_ref.shape[0]):
        term = term + part_ref[i] * factor[:, i : i + 1]
    term_s[...] = term
    span = term_s.shape[1] // n_cross
    per_row = 128 // span
    for c in range(n_cross):
        for r in range(rank):
            pieces[c, r // per_row : r // per_row + 1, (r % per_row) * span : (r % per_row + 1) * span] = (
                term_s[r : r + 1, c * span : (c + 1) * span])

    def send_loop_b(p, carry):
        @pl.when(p != me_b)
        def _():
            pltpu.make_async_remote_copy(
                src_ref=pieces.at[p % n_cross], dst_ref=recv_b.at[me_b],
                send_sem=send_b.at[p], recv_sem=got_b.at[me_b], device_id=peer_b(p), device_id_type=MESH,
            ).start()
        return carry

    def wait_loop_b(p, carry):
        @pl.when(p != me_b)
        def _():
            pltpu.make_async_remote_copy(
                src_ref=pieces.at[p % n_cross], dst_ref=recv_b.at[p],
                send_sem=send_b.at[p], recv_sem=got_b.at[p], device_id=peer_b(p), device_id_type=MESH,
            ).wait()
        return carry

    lax.fori_loop(0, group_b, send_loop_b, 0)
    recv_b[me_b] = pieces[cross]
    lax.fori_loop(0, group_b, wait_loop_b, 0)

    total = recv_b[0]
    for p in range(1, group_b):
        total = total + recv_b[p]
    total_s[...] = total * scale
    for r in range(rank):
        mode_ref[r : r + 1, :] = total_s[r // per_row : r // per_row + 1, (r % per_row) * span : (r % per_row + 1) * span]


def local(density, roll_start, mach_factor, cross_factor):
    rolls_here, bins_here, cross_here = density.shape
    rank = cross_factor.shape[0]
    n_roll = lax.axis_size("roll")
    n_mach = lax.axis_size("mach")
    n_cross = lax.axis_size("cross")
    n_chunks = 4
    pay_rows = 3 * rank * rank // 128
    span = bins_here // n_cross
    scale = rank / (rolls_here * n_roll * cross_here * n_cross)
    roll_factor, mode_two = pl.pallas_call(
        functools.partial(fused_kernel, n_roll, n_cross, scale, n_chunks),
        out_shape=(
            jax.ShapeDtypeStruct(roll_start.shape, jnp.float32),
            jax.ShapeDtypeStruct((rank, span), jnp.float32),
        ),
        in_specs=[pl.BlockSpec(memory_space=pl.ANY)] + [pl.BlockSpec(memory_space=VMEM)] * 3,
        out_specs=[pl.BlockSpec(memory_space=VMEM)] * 2,
        scratch_shapes=[
            VMEM(density.shape, density.dtype),
            pltpu.SemaphoreType.DMA((n_chunks,)),
            VMEM((rolls_here, rank, bins_here), jnp.float32),
            VMEM((3, rank, rank), jnp.float32),
            VMEM((pay_rows, 128), jnp.float32),
            VMEM((n_mach * n_cross, pay_rows, 128), jnp.float32),
            pltpu.SemaphoreType.DMA((n_mach * n_cross,)),
            pltpu.SemaphoreType.DMA((n_mach * n_cross,)),
            VMEM((rank, rank), jnp.float32),
            VMEM((rank, rank), jnp.float32),
            VMEM((rank, rank), jnp.float32),
            VMEM((rank, bins_here), jnp.float32),
            VMEM((n_cross, rank * span // 128, 128), jnp.float32),
            VMEM((n_roll * n_cross, rank * span // 128, 128), jnp.float32),
            pltpu.SemaphoreType.DMA((n_roll * n_cross,)),
            pltpu.SemaphoreType.DMA((n_roll * n_cross,)),
            VMEM((rank * span // 128, 128), jnp.float32),
        ],
        compiler_params=pltpu.CompilerParams(collective_id=0, has_side_effects=True),
    )(density, cross_factor, mach_factor, roll_start)
    return (roll_factor, mode_two)


def solution(mesh):
    in_specs = (P("roll", "mach", "cross"), P(None, "roll"), P(None, "mach"), P(None, "cross"))
    out_specs = (P(None, "roll"), P(None, ("mach", "cross")))
    return jax.shard_map(local, mesh=mesh, in_specs=in_specs, out_specs=out_specs, check_vma=False)
```

```python
import functools

import jax
import jax.numpy as jnp
from jax import lax
from jax.experimental import pallas as pl
from jax.experimental.pallas import tpu as pltpu
from jax.sharding import PartitionSpec as P

MESH = pl.DeviceIdType.MESH
VMEM = pltpu.VMEM


def fused_kernel(n_roll, n_cross, scale, n_chunks, dens_hbm, cross_ref, mach_ref, start_ref, rf_ref, mode_ref,
                 dens_v, dens_sem, part_ref, local_s, pay_ref,
                 recv_a, send_a, got_a, gm_s, mt_s, gc_s, term_s, pieces, recv_b, send_b, got_b, total_s):
    roll = lax.axis_index("roll")
    mach = lax.axis_index("mach")
    cross = lax.axis_index("cross")
    group_a = recv_a.shape[0]
    group_b = recv_b.shape[0]
    n_mach = group_a // n_cross
    me_a = mach * n_cross + cross
    me_b = roll * n_cross + cross
    rank = rf_ref.shape[0]

    def peer_a(p):
        return (roll, p // n_cross, p % n_cross)

    def peer_b(p):
        return (p // n_cross, mach, p % n_cross)

    rolls_here = dens_v.shape[0]
    chunk = rolls_here // n_chunks
    loads = [
        pltpu.make_async_copy(dens_hbm.at[pl.ds(k * chunk, chunk)], dens_v.at[pl.ds(k * chunk, chunk)], dens_sem.at[k])
        for k in range(n_chunks)
    ]
    for load in loads:
        load.start()

    barrier = pltpu.get_barrier_semaphore()

    def greet_a(p, carry):
        @pl.when(p != me_a)
        def _():
            pl.semaphore_signal(barrier, inc=1, device_id=peer_a(p), device_id_type=MESH)
        return carry

    def greet_b(p, carry):
        @pl.when(p // n_cross != roll)
        def _():
            pl.semaphore_signal(barrier, inc=1, device_id=peer_b(p), device_id_type=MESH)
        return carry

    lax.fori_loop(0, group_a, greet_a, 0)
    lax.fori_loop(0, group_b, greet_b, 0)

    nt = (((1,), (1,)), ((), ()))
    cross_f = cross_ref[...]
    mach_f = mach_ref[...]
    mach_w = mach_f.astype(jnp.float32)
    local_s[0] = lax.dot_general(mach_f, mach_f, nt, preferred_element_type=jnp.float32)
    local_s[2] = lax.dot_general(cross_f, cross_f, nt, preferred_element_type=jnp.float32)
    lane = lax.broadcasted_iota(jnp.int32, (rank, rolls_here), 1)
    terms_local = jnp.zeros((rank, rolls_here), jnp.float32)
    for k in range(n_chunks):
        loads[k].wait()
        for i in range(k * chunk, (k + 1) * chunk):
            value = lax.dot_general(cross_f, dens_v[i], nt, preferred_element_type=jnp.float32)
            part_ref[i] = value
            column = jnp.sum(value * mach_w, axis=1, keepdims=True)
            terms_local = jnp.where(lane == i, column, terms_local)
    local_s[1] = terms_local
    for k in range(3):
        for g in range(4):
            pay_ref[8 * k : 8 * k + 8, g * 32 : (g + 1) * 32] = local_s[k, pl.ds(g, 8, stride=4), :]

    pl.semaphore_wait(barrier, group_a - 1 + group_b - n_cross)

    def each_peer(p, action):
        pm = p // n_cross
        pc = p % n_cross

        @pl.when(jnp.logical_and(pc == cross, pm != mach))
        def _():
            action(p, 0, 16)

        @pl.when(jnp.logical_and(pm == mach, pc != cross))
        def _():
            action(p, 8, 16)

        @pl.when(jnp.logical_and(pm != mach, pc != cross))
        def _():
            action(p, 8, 8)

    def start_a(p, lo, size):
        pltpu.make_async_remote_copy(
            src_ref=pay_ref.at[pl.ds(lo, size)], dst_ref=recv_a.at[me_a, pl.ds(lo, size)],
            send_sem=send_a.at[p], recv_sem=got_a.at[me_a], device_id=peer_a(p), device_id_type=MESH,
        ).start()

    def finish_a(p, lo, size):
        pltpu.make_async_remote_copy(
            src_ref=pay_ref.at[pl.ds(lo, size)], dst_ref=recv_a.at[p, pl.ds(lo, size)],
            send_sem=send_a.at[p], recv_sem=got_a.at[p], device_id=peer_a(p), device_id_type=MESH,
        ).wait()

    def send_loop_a(p, carry):
        each_peer(p, start_a)
        return carry

    def wait_loop_a(p, carry):
        each_peer(p, finish_a)
        return carry

    lax.fori_loop(0, group_a, send_loop_a, 0)
    recv_a[me_a] = pay_ref[...]
    lax.fori_loop(0, group_a, wait_loop_a, 0)

    terms = recv_a[0, 8:16, :]
    for p in range(1, group_a):
        terms = terms + recv_a[p, 8:16, :]
    gm = recv_a[cross, 0:8, :]
    for q in range(1, n_mach):
        gm = gm + recv_a[q * n_cross + cross, 0:8, :]
    gc = recv_a[mach * n_cross, 16:24, :]
    for q in range(1, n_cross):
        gc = gc + recv_a[mach * n_cross + q, 16:24, :]
    for g in range(4):
        lanes = slice(g * 32, (g + 1) * 32)
        gm_s[pl.ds(g, 8, stride=4), :] = gm[:, lanes]
        mt_s[pl.ds(g, 8, stride=4), :] = terms[:, lanes]
        gc_s[pl.ds(g, 8, stride=4), :] = gc[:, lanes]

    gram = gm_s[...] * gc_s[...]
    target = mt_s[...]
    rows = start_ref[...]
    mixed = gram[:, 0:1] * rows[0:1, :]
    for s_ in range(1, rank):
        mixed = mixed + gram[:, s_ : s_ + 1] * rows[s_ : s_ + 1, :]
    for r in range(rank):
        current = rows[r : r + 1, :]
        updated = jnp.maximum(current + (target[r : r + 1, :] - mixed[r : r + 1, :]) / gram[r : r + 1, r : r + 1], 0.0)
        rf_ref[r : r + 1, :] = updated
        mixed = mixed + gram[:, r : r + 1] * (updated - current)

    factor = rf_ref[...]
    term = part_ref[0] * factor[:, 0:1]
    for i in range(1, part_ref.shape[0]):
        term = term + part_ref[i] * factor[:, i : i + 1]
    term_s[...] = term
    span = term_s.shape[1] // n_cross
    per_row = 128 // span
    for c in range(n_cross):
        for r in range(rank):
            pieces[c, r // per_row : r // per_row + 1, (r % per_row) * span : (r % per_row + 1) * span] = (
                term_s[r : r + 1, c * span : (c + 1) * span])

    def send_loop_b(p, carry):
        @pl.when(p != me_b)
        def _():
            pltpu.make_async_remote_copy(
                src_ref=pieces.at[p % n_cross], dst_ref=recv_b.at[me_b],
                send_sem=send_b.at[p], recv_sem=got_b.at[me_b], device_id=peer_b(p), device_id_type=MESH,
            ).start()
        return carry

    def wait_loop_b(p, carry):
        @pl.when(p != me_b)
        def _():
            pltpu.make_async_remote_copy(
                src_ref=pieces.at[p % n_cross], dst_ref=recv_b.at[p],
                send_sem=send_b.at[p], recv_sem=got_b.at[p], device_id=peer_b(p), device_id_type=MESH,
            ).wait()
        return carry

    lax.fori_loop(0, group_b, send_loop_b, 0)
    recv_b[me_b] = pieces[cross]
    lax.fori_loop(0, group_b, wait_loop_b, 0)

    total = recv_b[0]
    for p in range(1, group_b):
        total = total + recv_b[p]
    total_s[...] = total * scale
    for r in range(rank):
        mode_ref[r : r + 1, :] = total_s[r // per_row : r // per_row + 1, (r % per_row) * span : (r % per_row + 1) * span]


def local(density, roll_start, mach_factor, cross_factor):
    rolls_here, bins_here, cross_here = density.shape
    rank = cross_factor.shape[0]
    n_roll = lax.axis_size("roll")
    n_mach = lax.axis_size("mach")
    n_cross = lax.axis_size("cross")
    n_chunks = 4
    pay_rows = 3 * rank * rank // 128
    span = bins_here // n_cross
    scale = rank / (rolls_here * n_roll * cross_here * n_cross)
    roll_factor, mode_two = pl.pallas_call(
        functools.partial(fused_kernel, n_roll, n_cross, scale, n_chunks),
        out_shape=(
            jax.ShapeDtypeStruct(roll_start.shape, jnp.float32),
            jax.ShapeDtypeStruct((rank, span), jnp.float32),
        ),
        in_specs=[pl.BlockSpec(memory_space=pl.ANY)] + [pl.BlockSpec(memory_space=VMEM)] * 3,
        out_specs=[pl.BlockSpec(memory_space=VMEM)] * 2,
        scratch_shapes=[
            VMEM(density.shape, density.dtype),
            pltpu.SemaphoreType.DMA((n_chunks,)),
            VMEM((rolls_here, rank, bins_here), jnp.float32),
            VMEM((3, rank, rank), jnp.float32),
            VMEM((pay_rows, 128), jnp.float32),
            VMEM((n_mach * n_cross, pay_rows, 128), jnp.float32),
            pltpu.SemaphoreType.DMA((n_mach * n_cross,)),
            pltpu.SemaphoreType.DMA((n_mach * n_cross,)),
            VMEM((rank, rank), jnp.float32),
            VMEM((rank, rank), jnp.float32),
            VMEM((rank, rank), jnp.float32),
            VMEM((rank, bins_here), jnp.float32),
            VMEM((n_cross, rank * span // 128, 128), jnp.float32),
            VMEM((n_roll * n_cross, rank * span // 128, 128), jnp.float32),
            pltpu.SemaphoreType.DMA((n_roll * n_cross,)),
            pltpu.SemaphoreType.DMA((n_roll * n_cross,)),
            VMEM((rank * span // 128, 128), jnp.float32),
        ],
        compiler_params=pltpu.CompilerParams(collective_id=0, has_side_effects=True),
    )(density, cross_factor, mach_factor, roll_start)
    return (roll_factor, mode_two)


def solution(mesh):
    in_specs = (P("roll", "mach", "cross"), P(None, "roll"), P(None, "mach"), P(None, "cross"))
    out_specs = (P(None, "roll"), P(None, ("mach", "cross")))
    return jax.shard_map(local, mesh=mesh, in_specs=in_specs, out_specs=out_specs, check_vma=False)
```

```python
import functools

import jax
import jax.numpy as jnp
from jax import lax
from jax.experimental import pallas as pl
from jax.experimental.pallas import tpu as pltpu
from jax.sharding import PartitionSpec as P

MESH = pl.DeviceIdType.MESH
VMEM = pltpu.VMEM


def fused_kernel(n_roll, n_cross, scale, n_chunks, dens_hbm, cross_ref, mach_ref, start_ref, rf_ref, mode_ref,
                 dens_v, dens_sem, part_ref, local_s, pay_ref,
                 recv_a, send_a, got_a, gm_s, mt_s, gc_s, term_s, pieces, recv_b, send_b, got_b, total_s):
    roll = lax.axis_index("roll")
    mach = lax.axis_index("mach")
    cross = lax.axis_index("cross")
    group_a = recv_a.shape[0]
    group_b = recv_b.shape[0]
    n_mach = group_a // n_cross
    me_a = mach * n_cross + cross
    me_b = roll * n_cross + cross
    rank = rf_ref.shape[0]

    def peer_a(p):
        return (roll, p // n_cross, p % n_cross)

    def peer_b(p):
        return (p // n_cross, mach, p % n_cross)

    rolls_here = dens_v.shape[0]
    chunk = rolls_here // n_chunks
    loads = [
        pltpu.make_async_copy(dens_hbm.at[pl.ds(k * chunk, chunk)], dens_v.at[pl.ds(k * chunk, chunk)], dens_sem.at[k])
        for k in range(n_chunks)
    ]
    for load in loads:
        load.start()

    barrier = pltpu.get_barrier_semaphore()

    def greet_a(p, carry):
        @pl.when(p != me_a)
        def _():
            pl.semaphore_signal(barrier, inc=1, device_id=peer_a(p), device_id_type=MESH)
        return carry

    def greet_b(p, carry):
        @pl.when(p // n_cross != roll)
        def _():
            pl.semaphore_signal(barrier, inc=1, device_id=peer_b(p), device_id_type=MESH)
        return carry

    lax.fori_loop(0, group_a, greet_a, 0)
    lax.fori_loop(0, group_b, greet_b, 0)

    nt = (((1,), (1,)), ((), ()))
    cross_f = cross_ref[...]
    mach_f = mach_ref[...]
    mach_w = mach_f.astype(jnp.float32)
    local_s[0] = lax.dot_general(mach_f, mach_f, nt, preferred_element_type=jnp.float32)
    local_s[2] = lax.dot_general(cross_f, cross_f, nt, preferred_element_type=jnp.float32)
    for k in (0, 2):
        for g in range(4):
            pay_ref[8 * k : 8 * k + 8, g * 32 : (g + 1) * 32] = local_s[k, pl.ds(g, 8, stride=4), :]

    def start_rows(p, lo, size):
        pltpu.make_async_remote_copy(
            src_ref=pay_ref.at[pl.ds(lo, size)], dst_ref=recv_a.at[me_a, pl.ds(lo, size)],
            send_sem=send_a.at[p], recv_sem=got_a.at[me_a], device_id=peer_a(p), device_id_type=MESH,
        ).start()

    def send_grams(p, carry):
        pm = p // n_cross
        pc = p % n_cross

        @pl.when(jnp.logical_and(pc == cross, pm != mach))
        def _():
            start_rows(p, 0, 8)

        @pl.when(jnp.logical_and(pm == mach, pc != cross))
        def _():
            start_rows(p, 16, 8)
        return carry

    chunk_rows = chunk * rank // 128

    def send_chunk(k):
        def body(p, carry):
            @pl.when(p != me_a)
            def _():
                start_rows(p, 8 + k * chunk_rows, chunk_rows)
            return carry
        lax.fori_loop(0, group_a, body, 0)

    lane = lax.broadcasted_iota(jnp.int32, (rank, rolls_here), 1)
    terms_local = jnp.zeros((rank, rolls_here), jnp.float32)
    wait_after = max(n_chunks - 2, 0)
    for k in range(n_chunks):
        loads[k].wait()
        for i in range(k * chunk, (k + 1) * chunk):
            value = lax.dot_general(cross_f, dens_v[i], nt, preferred_element_type=jnp.float32)
            part_ref[i] = value
            column = jnp.sum(value * mach_w, axis=1, keepdims=True)
            terms_local = jnp.where(lane == i, column, terms_local)
        local_s[1] = terms_local.T
        for h in range(chunk_rows):
            for g in range(4):
                pay_ref[8 + k * chunk_rows + h : 9 + k * chunk_rows + h, g * 32 : (g + 1) * 32] = (
                    local_s[1, k * chunk + 4 * h + g : k * chunk + 4 * h + g + 1, :])
        if k == wait_after:
            pl.semaphore_wait(barrier, group_a - 1 + group_b - n_cross)
            lax.fori_loop(0, group_a, send_grams, 0)
            for c in range(k + 1):
                send_chunk(c)
        elif k > wait_after:
            send_chunk(k)

    def each_peer(p, action):
        pm = p // n_cross
        pc = p % n_cross

        @pl.when(jnp.logical_and(pc == cross, pm != mach))
        def _():
            action(p, 0, 16)

        @pl.when(jnp.logical_and(pm == mach, pc != cross))
        def _():
            action(p, 8, 16)

        @pl.when(jnp.logical_and(pm != mach, pc != cross))
        def _():
            action(p, 8, 8)

    def finish_a(p, lo, size):
        pltpu.make_async_remote_copy(
            src_ref=pay_ref.at[pl.ds(lo, size)], dst_ref=recv_a.at[p, pl.ds(lo, size)],
            send_sem=send_a.at[p], recv_sem=got_a.at[p], device_id=peer_a(p), device_id_type=MESH,
        ).wait()

    def wait_loop_a(p, carry):
        each_peer(p, finish_a)
        return carry

    recv_a[me_a] = pay_ref[...]
    lax.fori_loop(0, group_a, wait_loop_a, 0)

    terms = recv_a[0, 8:16, :]
    for p in range(1, group_a):
        terms = terms + recv_a[p, 8:16, :]
    gm = recv_a[cross, 0:8, :]
    for q in range(1, n_mach):
        gm = gm + recv_a[q * n_cross + cross, 0:8, :]
    gc = recv_a[mach * n_cross, 16:24, :]
    for q in range(1, n_cross):
        gc = gc + recv_a[mach * n_cross + q, 16:24, :]
    for g in range(4):
        lanes = slice(g * 32, (g + 1) * 32)
        gm_s[pl.ds(g, 8, stride=4), :] = gm[:, lanes]
        mt_s[pl.ds(g, 8, stride=4), :] = terms[:, lanes]
        gc_s[pl.ds(g, 8, stride=4), :] = gc[:, lanes]

    gram = gm_s[...] * gc_s[...]
    target = mt_s[...].T
    rows = start_ref[...]
    mixed = gram[:, 0:1] * rows[0:1, :]
    for s_ in range(1, rank):
        mixed = mixed + gram[:, s_ : s_ + 1] * rows[s_ : s_ + 1, :]
    for r in range(rank):
        current = rows[r : r + 1, :]
        updated = jnp.maximum(current + (target[r : r + 1, :] - mixed[r : r + 1, :]) / gram[r : r + 1, r : r + 1], 0.0)
        rf_ref[r : r + 1, :] = updated
        mixed = mixed + gram[:, r : r + 1] * (updated - current)

    factor = rf_ref[...]
    term = part_ref[0] * factor[:, 0:1]
    for i in range(1, part_ref.shape[0]):
        term = term + part_ref[i] * factor[:, i : i + 1]
    term_s[...] = term
    span = term_s.shape[1] // n_cross
    per_row = 128 // span
    for c in range(n_cross):
        for r in range(rank):
            pieces[c, r // per_row : r // per_row + 1, (r % per_row) * span : (r % per_row + 1) * span] = (
                term_s[r : r + 1, c * span : (c + 1) * span])

    def send_loop_b(p, carry):
        @pl.when(p != me_b)
        def _():
            pltpu.make_async_remote_copy(
                src_ref=pieces.at[p % n_cross], dst_ref=recv_b.at[me_b],
                send_sem=send_b.at[p], recv_sem=got_b.at[me_b], device_id=peer_b(p), device_id_type=MESH,
            ).start()
        return carry

    def wait_loop_b(p, carry):
        @pl.when(p != me_b)
        def _():
            pltpu.make_async_remote_copy(
                src_ref=pieces.at[p % n_cross], dst_ref=recv_b.at[p],
                send_sem=send_b.at[p], recv_sem=got_b.at[p], device_id=peer_b(p), device_id_type=MESH,
            ).wait()
        return carry

    lax.fori_loop(0, group_b, send_loop_b, 0)
    recv_b[me_b] = pieces[cross]
    lax.fori_loop(0, group_b, wait_loop_b, 0)

    total = recv_b[0]
    for p in range(1, group_b):
        total = total + recv_b[p]
    total_s[...] = total * scale
    for r in range(rank):
        mode_ref[r : r + 1, :] = total_s[r // per_row : r // per_row + 1, (r % per_row) * span : (r % per_row + 1) * span]


def local(density, roll_start, mach_factor, cross_factor):
    rolls_here, bins_here, cross_here = density.shape
    rank = cross_factor.shape[0]
    n_roll = lax.axis_size("roll")
    n_mach = lax.axis_size("mach")
    n_cross = lax.axis_size("cross")
    n_chunks = 4
    pay_rows = 3 * rank * rank // 128
    span = bins_here // n_cross
    scale = rank / (rolls_here * n_roll * cross_here * n_cross)
    roll_factor, mode_two = pl.pallas_call(
        functools.partial(fused_kernel, n_roll, n_cross, scale, n_chunks),
        out_shape=(
            jax.ShapeDtypeStruct(roll_start.shape, jnp.float32),
            jax.ShapeDtypeStruct((rank, span), jnp.float32),
        ),
        in_specs=[pl.BlockSpec(memory_space=pl.ANY)] + [pl.BlockSpec(memory_space=VMEM)] * 3,
        out_specs=[pl.BlockSpec(memory_space=VMEM)] * 2,
        scratch_shapes=[
            VMEM(density.shape, density.dtype),
            pltpu.SemaphoreType.DMA((n_chunks,)),
            VMEM((rolls_here, rank, bins_here), jnp.float32),
            VMEM((3, rank, rank), jnp.float32),
            VMEM((pay_rows, 128), jnp.float32),
            VMEM((n_mach * n_cross, pay_rows, 128), jnp.float32),
            pltpu.SemaphoreType.DMA((n_mach * n_cross,)),
            pltpu.SemaphoreType.DMA((n_mach * n_cross,)),
            VMEM((rank, rank), jnp.float32),
            VMEM((rank, rank), jnp.float32),
            VMEM((rank, rank), jnp.float32),
            VMEM((rank, bins_here), jnp.float32),
            VMEM((n_cross, rank * span // 128, 128), jnp.float32),
            VMEM((n_roll * n_cross, rank * span // 128, 128), jnp.float32),
            pltpu.SemaphoreType.DMA((n_roll * n_cross,)),
            pltpu.SemaphoreType.DMA((n_roll * n_cross,)),
            VMEM((rank * span // 128, 128), jnp.float32),
        ],
        compiler_params=pltpu.CompilerParams(collective_id=0, has_side_effects=True),
    )(density, cross_factor, mach_factor, roll_start)
    return (roll_factor, mode_two)


def solution(mesh):
    in_specs = (P("roll", "mach", "cross"), P(None, "roll"), P(None, "mach"), P(None, "cross"))
    out_specs = (P(None, "roll"), P(None, ("mach", "cross")))
    return jax.shard_map(local, mesh=mesh, in_specs=in_specs, out_specs=out_specs, check_vma=False)
```

```python
import functools

import jax
import jax.numpy as jnp
from jax import lax
from jax.experimental import pallas as pl
from jax.experimental.pallas import tpu as pltpu
from jax.sharding import PartitionSpec as P

MESH = pl.DeviceIdType.MESH
VMEM = pltpu.VMEM


def fused_kernel(n_roll, n_cross, scale, n_chunks, dens_hbm, cross_ref, mach_ref, start_ref, rf_ref, mode_ref,
                 dens_v, dens_sem, part_ref, local_s, pay_ref,
                 recv_1, send_1, got_1, pay_2, recv_2, send_2, got_2, gm_s, mt_s, gc_s, term_s, pieces, recv_b, send_b, got_b, total_s):
    roll = lax.axis_index("roll")
    mach = lax.axis_index("mach")
    cross = lax.axis_index("cross")
    n_mach = recv_2.shape[0]
    group_b = recv_b.shape[0]
    me_b = roll * n_cross + cross
    rank = rf_ref.shape[0]

    def peer_c(p):
        return (roll, mach, p)

    def peer_m(p):
        return (roll, p, cross)

    def peer_b(p):
        return (p // n_cross, mach, p % n_cross)

    rolls_here = dens_v.shape[0]
    chunk = rolls_here // n_chunks
    loads = [
        pltpu.make_async_copy(dens_hbm.at[pl.ds(k * chunk, chunk)], dens_v.at[pl.ds(k * chunk, chunk)], dens_sem.at[k])
        for k in range(n_chunks)
    ]
    for load in loads:
        load.start()

    barrier = pltpu.get_barrier_semaphore()

    def greet_m(p, carry):
        @pl.when(p != mach)
        def _():
            pl.semaphore_signal(barrier, inc=1, device_id=peer_m(p), device_id_type=MESH)
        return carry

    def greet_b(p, carry):
        @pl.when(p // n_cross != roll)
        def _():
            pl.semaphore_signal(barrier, inc=1, device_id=peer_b(p), device_id_type=MESH)
        return carry

    lax.fori_loop(0, n_mach, greet_m, 0)
    for p in range(n_cross):
        @pl.when(p != cross)
        def _():
            pl.semaphore_signal(barrier, inc=1, device_id=peer_c(p), device_id_type=MESH)
    lax.fori_loop(0, group_b, greet_b, 0)

    nt = (((1,), (1,)), ((), ()))
    cross_f = cross_ref[...]
    mach_f = mach_ref[...]
    mach_w = mach_f.astype(jnp.float32)
    local_s[0] = lax.dot_general(mach_f, mach_f, nt, preferred_element_type=jnp.float32)
    local_s[2] = lax.dot_general(cross_f, cross_f, nt, preferred_element_type=jnp.float32)
    lane = lax.broadcasted_iota(jnp.int32, (rank, rolls_here), 1)
    terms_local = jnp.zeros((rank, rolls_here), jnp.float32)
    for k in range(n_chunks):
        loads[k].wait()
        for i in range(k * chunk, (k + 1) * chunk):
            value = lax.dot_general(cross_f, dens_v[i], nt, preferred_element_type=jnp.float32)
            part_ref[i] = value
            column = jnp.sum(value * mach_w, axis=1, keepdims=True)
            terms_local = jnp.where(lane == i, column, terms_local)
    local_s[1] = terms_local
    for k in range(3):
        for g in range(4):
            pay_ref[8 * k : 8 * k + 8, g * 32 : (g + 1) * 32] = local_s[k, pl.ds(g, 8, stride=4), :]

    pl.semaphore_wait(barrier, n_mach - 1 + group_b - 1)

    def stage_1(p):
        return pltpu.make_async_remote_copy(
            src_ref=pay_ref.at[pl.ds(8, 16)], dst_ref=recv_1.at[cross], send_sem=send_1.at[p],
            recv_sem=got_1.at[cross], device_id=peer_c(p), device_id_type=MESH)

    def stage_1_in(p):
        return pltpu.make_async_remote_copy(
            src_ref=pay_ref.at[pl.ds(8, 16)], dst_ref=recv_1.at[p], send_sem=send_1.at[p],
            recv_sem=got_1.at[p], device_id=peer_c(p), device_id_type=MESH)

    for p in range(n_cross):
        @pl.when(p != cross)
        def _():
            stage_1(p).start()
    recv_1[cross] = pay_ref[8:24, :]
    for p in range(n_cross):
        @pl.when(p != cross)
        def _():
            stage_1_in(p).wait()
    terms = recv_1[0, 0:8, :]
    gc = recv_1[0, 8:16, :]
    for p in range(1, n_cross):
        terms = terms + recv_1[p, 0:8, :]
        gc = gc + recv_1[p, 8:16, :]

    pay_2[0:8, :] = pay_ref[0:8, :]
    pay_2[8:16, :] = terms

    def send_loop_2(p, carry):
        @pl.when(p != mach)
        def _():
            pltpu.make_async_remote_copy(
                src_ref=pay_2, dst_ref=recv_2.at[mach], send_sem=send_2.at[p], recv_sem=got_2.at[mach],
                device_id=peer_m(p), device_id_type=MESH).start()
        return carry

    def wait_loop_2(p, carry):
        @pl.when(p != mach)
        def _():
            pltpu.make_async_remote_copy(
                src_ref=pay_2, dst_ref=recv_2.at[p], send_sem=send_2.at[p], recv_sem=got_2.at[p],
                device_id=peer_m(p), device_id_type=MESH).wait()
        return carry

    lax.fori_loop(0, n_mach, send_loop_2, 0)
    recv_2[mach] = pay_2[...]
    lax.fori_loop(0, n_mach, wait_loop_2, 0)
    gm = recv_2[0, 0:8, :]
    terms = recv_2[0, 8:16, :]
    for p in range(1, n_mach):
        gm = gm + recv_2[p, 0:8, :]
        terms = terms + recv_2[p, 8:16, :]
    for g in range(4):
        lanes = slice(g * 32, (g + 1) * 32)
        gm_s[pl.ds(g, 8, stride=4), :] = gm[:, lanes]
        mt_s[pl.ds(g, 8, stride=4), :] = terms[:, lanes]
        gc_s[pl.ds(g, 8, stride=4), :] = gc[:, lanes]

    gram = gm_s[...] * gc_s[...]
    target = mt_s[...]
    rows = start_ref[...]
    mixed = gram[:, 0:1] * rows[0:1, :]
    for s_ in range(1, rank):
        mixed = mixed + gram[:, s_ : s_ + 1] * rows[s_ : s_ + 1, :]
    for r in range(rank):
        current = rows[r : r + 1, :]
        updated = jnp.maximum(current + (target[r : r + 1, :] - mixed[r : r + 1, :]) / gram[r : r + 1, r : r + 1], 0.0)
        rf_ref[r : r + 1, :] = updated
        mixed = mixed + gram[:, r : r + 1] * (updated - current)

    factor = rf_ref[...]
    term = part_ref[0] * factor[:, 0:1]
    for i in range(1, part_ref.shape[0]):
        term = term + part_ref[i] * factor[:, i : i + 1]
    term_s[...] = term
    span = term_s.shape[1] // n_cross
    per_row = 128 // span
    for c in range(n_cross):
        for r in range(rank):
            pieces[c, r // per_row : r // per_row + 1, (r % per_row) * span : (r % per_row + 1) * span] = (
                term_s[r : r + 1, c * span : (c + 1) * span])

    def send_loop_b(p, carry):
        @pl.when(p != me_b)
        def _():
            pltpu.make_async_remote_copy(
                src_ref=pieces.at[p % n_cross], dst_ref=recv_b.at[me_b],
                send_sem=send_b.at[p], recv_sem=got_b.at[me_b], device_id=peer_b(p), device_id_type=MESH,
            ).start()
        return carry

    def wait_loop_b(p, carry):
        @pl.when(p != me_b)
        def _():
            pltpu.make_async_remote_copy(
                src_ref=pieces.at[p % n_cross], dst_ref=recv_b.at[p],
                send_sem=send_b.at[p], recv_sem=got_b.at[p], device_id=peer_b(p), device_id_type=MESH,
            ).wait()
        return carry

    lax.fori_loop(0, group_b, send_loop_b, 0)
    recv_b[me_b] = pieces[cross]
    lax.fori_loop(0, group_b, wait_loop_b, 0)

    total = recv_b[0]
    for p in range(1, group_b):
        total = total + recv_b[p]
    total_s[...] = total * scale
    for r in range(rank):
        mode_ref[r : r + 1, :] = total_s[r // per_row : r // per_row + 1, (r % per_row) * span : (r % per_row + 1) * span]


def local(density, roll_start, mach_factor, cross_factor):
    rolls_here, bins_here, cross_here = density.shape
    rank = cross_factor.shape[0]
    n_roll = lax.axis_size("roll")
    n_mach = lax.axis_size("mach")
    n_cross = lax.axis_size("cross")
    n_chunks = 4
    pay_rows = 3 * rank * rank // 128
    span = bins_here // n_cross
    scale = rank / (rolls_here * n_roll * cross_here * n_cross)
    roll_factor, mode_two = pl.pallas_call(
        functools.partial(fused_kernel, n_roll, n_cross, scale, n_chunks),
        out_shape=(
            jax.ShapeDtypeStruct(roll_start.shape, jnp.float32),
            jax.ShapeDtypeStruct((rank, span), jnp.float32),
        ),
        in_specs=[pl.BlockSpec(memory_space=pl.ANY)] + [pl.BlockSpec(memory_space=VMEM)] * 3,
        out_specs=[pl.BlockSpec(memory_space=VMEM)] * 2,
        scratch_shapes=[
            VMEM(density.shape, density.dtype),
            pltpu.SemaphoreType.DMA((n_chunks,)),
            VMEM((rolls_here, rank, bins_here), jnp.float32),
            VMEM((3, rank, rank), jnp.float32),
            VMEM((pay_rows, 128), jnp.float32),
            VMEM((n_cross, 16, 128), jnp.float32),
            pltpu.SemaphoreType.DMA((n_cross,)),
            pltpu.SemaphoreType.DMA((n_cross,)),
            VMEM((16, 128), jnp.float32),
            VMEM((n_mach, 16, 128), jnp.float32),
            pltpu.SemaphoreType.DMA((n_mach,)),
            pltpu.SemaphoreType.DMA((n_mach,)),
            VMEM((rank, rank), jnp.float32),
            VMEM((rank, rank), jnp.float32),
            VMEM((rank, rank), jnp.float32),
            VMEM((rank, bins_here), jnp.float32),
            VMEM((n_cross, rank * span // 128, 128), jnp.float32),
            VMEM((n_roll * n_cross, rank * span // 128, 128), jnp.float32),
            pltpu.SemaphoreType.DMA((n_roll * n_cross,)),
            pltpu.SemaphoreType.DMA((n_roll * n_cross,)),
            VMEM((rank * span // 128, 128), jnp.float32),
        ],
        compiler_params=pltpu.CompilerParams(collective_id=0, has_side_effects=True),
    )(density, cross_factor, mach_factor, roll_start)
    return (roll_factor, mode_two)


def solution(mesh):
    in_specs = (P("roll", "mach", "cross"), P(None, "roll"), P(None, "mach"), P(None, "cross"))
    out_specs = (P(None, "roll"), P(None, ("mach", "cross")))
    return jax.shard_map(local, mesh=mesh, in_specs=in_specs, out_specs=out_specs, check_vma=False)
```

```python
import functools

import jax
import jax.numpy as jnp
from jax import lax
from jax.experimental import pallas as pl
from jax.experimental.pallas import tpu as pltpu
from jax.sharding import PartitionSpec as P

MESH = pl.DeviceIdType.MESH
VMEM = pltpu.VMEM


def fused_kernel(n_roll, n_cross, scale, n_chunks, dens_hbm, cross_ref, mach_ref, start_ref, rf_ref, mode_ref,
                 dens_v, dens_sem, part_ref, local_s, pay_ref,
                 recv_1, send_1, got_1, pay_2, recv_2, send_2, got_2, pay_3, recv_3, send_3, got_3, gm_s, mt_s, gc_s, term_s, pieces, recv_b, send_b, got_b, total_s):
    roll = lax.axis_index("roll")
    mach = lax.axis_index("mach")
    cross = lax.axis_index("cross")
    n_x = recv_2.shape[0]
    n_y = recv_3.shape[0]
    mach_y = mach // n_x
    mach_x = mach % n_x
    group_b = recv_b.shape[0]
    me_b = roll * n_cross + cross
    rank = rf_ref.shape[0]

    def peer_c(p):
        return (roll, mach, p)

    def peer_x(p):
        return (roll, mach_y * n_x + p, cross)

    def peer_y(p):
        return (roll, p * n_x + mach_x, cross)

    def exchange(src_ref, recv_ref, send_sem, recv_sem, me, peer):
        for p in range(recv_ref.shape[0]):
            @pl.when(p != me)
            def _():
                pltpu.make_async_remote_copy(
                    src_ref=src_ref, dst_ref=recv_ref.at[me], send_sem=send_sem.at[p], recv_sem=recv_sem.at[me],
                    device_id=peer(p), device_id_type=MESH).start()
        recv_ref[me] = src_ref[...]
        for p in range(recv_ref.shape[0]):
            @pl.when(p != me)
            def _():
                pltpu.make_async_remote_copy(
                    src_ref=src_ref, dst_ref=recv_ref.at[p], send_sem=send_sem.at[p], recv_sem=recv_sem.at[p],
                    device_id=peer(p), device_id_type=MESH).wait()

    def peer_b(p):
        return (p // n_cross, mach, p % n_cross)

    rolls_here = dens_v.shape[0]
    chunk = rolls_here // n_chunks
    loads = [
        pltpu.make_async_copy(dens_hbm.at[pl.ds(k * chunk, chunk)], dens_v.at[pl.ds(k * chunk, chunk)], dens_sem.at[k])
        for k in range(n_chunks)
    ]
    for load in loads:
        load.start()

    barrier = pltpu.get_barrier_semaphore()


    def greet_b(p, carry):
        @pl.when(p // n_cross != roll)
        def _():
            pl.semaphore_signal(barrier, inc=1, device_id=peer_b(p), device_id_type=MESH)
        return carry

    for n, me, peer in ((n_cross, cross, peer_c), (n_x, mach_x, peer_x), (n_y, mach_y, peer_y)):
        for p in range(n):
            @pl.when(p != me)
            def _():
                pl.semaphore_signal(barrier, inc=1, device_id=peer(p), device_id_type=MESH)
    lax.fori_loop(0, group_b, greet_b, 0)

    nt = (((1,), (1,)), ((), ()))
    cross_f = cross_ref[...]
    mach_f = mach_ref[...]
    mach_w = mach_f.astype(jnp.float32)
    local_s[0] = lax.dot_general(mach_f, mach_f, nt, preferred_element_type=jnp.float32)
    local_s[2] = lax.dot_general(cross_f, cross_f, nt, preferred_element_type=jnp.float32)
    lane = lax.broadcasted_iota(jnp.int32, (rank, rolls_here), 1)
    terms_local = jnp.zeros((rank, rolls_here), jnp.float32)
    for k in range(n_chunks):
        loads[k].wait()
        for i in range(k * chunk, (k + 1) * chunk):
            value = lax.dot_general(cross_f, dens_v[i], nt, preferred_element_type=jnp.float32)
            part_ref[i] = value
            column = jnp.sum(value * mach_w, axis=1, keepdims=True)
            terms_local = jnp.where(lane == i, column, terms_local)
    local_s[1] = terms_local
    for k in range(3):
        for g in range(4):
            pay_ref[8 * k : 8 * k + 8, g * 32 : (g + 1) * 32] = local_s[k, pl.ds(g, 8, stride=4), :]

    pl.semaphore_wait(barrier, n_x - 1 + n_y - 1 + group_b - 1)

    def stage_1(p):
        return pltpu.make_async_remote_copy(
            src_ref=pay_ref.at[pl.ds(8, 16)], dst_ref=recv_1.at[cross], send_sem=send_1.at[p],
            recv_sem=got_1.at[cross], device_id=peer_c(p), device_id_type=MESH)

    def stage_1_in(p):
        return pltpu.make_async_remote_copy(
            src_ref=pay_ref.at[pl.ds(8, 16)], dst_ref=recv_1.at[p], send_sem=send_1.at[p],
            recv_sem=got_1.at[p], device_id=peer_c(p), device_id_type=MESH)

    for p in range(n_cross):
        @pl.when(p != cross)
        def _():
            stage_1(p).start()
    recv_1[cross] = pay_ref[8:24, :]
    for p in range(n_cross):
        @pl.when(p != cross)
        def _():
            stage_1_in(p).wait()
    terms = recv_1[0, 0:8, :]
    gc = recv_1[0, 8:16, :]
    for p in range(1, n_cross):
        terms = terms + recv_1[p, 0:8, :]
        gc = gc + recv_1[p, 8:16, :]

    pay_2[0:8, :] = pay_ref[0:8, :]
    pay_2[8:16, :] = terms
    exchange(pay_2, recv_2, send_2, got_2, mach_x, peer_x)
    gm = recv_2[0, 0:8, :]
    terms = recv_2[0, 8:16, :]
    for p in range(1, n_x):
        gm = gm + recv_2[p, 0:8, :]
        terms = terms + recv_2[p, 8:16, :]
    pay_3[0:8, :] = gm
    pay_3[8:16, :] = terms
    exchange(pay_3, recv_3, send_3, got_3, mach_y, peer_y)
    gm = recv_3[0, 0:8, :]
    terms = recv_3[0, 8:16, :]
    for p in range(1, n_y):
        gm = gm + recv_3[p, 0:8, :]
        terms = terms + recv_3[p, 8:16, :]
    for g in range(4):
        lanes = slice(g * 32, (g + 1) * 32)
        gm_s[pl.ds(g, 8, stride=4), :] = gm[:, lanes]
        mt_s[pl.ds(g, 8, stride=4), :] = terms[:, lanes]
        gc_s[pl.ds(g, 8, stride=4), :] = gc[:, lanes]

    gram = gm_s[...] * gc_s[...]
    target = mt_s[...]
    rows = start_ref[...]
    mixed = gram[:, 0:1] * rows[0:1, :]
    for s_ in range(1, rank):
        mixed = mixed + gram[:, s_ : s_ + 1] * rows[s_ : s_ + 1, :]
    for r in range(rank):
        current = rows[r : r + 1, :]
        updated = jnp.maximum(current + (target[r : r + 1, :] - mixed[r : r + 1, :]) / gram[r : r + 1, r : r + 1], 0.0)
        rf_ref[r : r + 1, :] = updated
        mixed = mixed + gram[:, r : r + 1] * (updated - current)

    factor = rf_ref[...]
    term = part_ref[0] * factor[:, 0:1]
    for i in range(1, part_ref.shape[0]):
        term = term + part_ref[i] * factor[:, i : i + 1]
    term_s[...] = term
    span = term_s.shape[1] // n_cross
    per_row = 128 // span
    for c in range(n_cross):
        for r in range(rank):
            pieces[c, r // per_row : r // per_row + 1, (r % per_row) * span : (r % per_row + 1) * span] = (
                term_s[r : r + 1, c * span : (c + 1) * span])

    def send_loop_b(p, carry):
        @pl.when(p != me_b)
        def _():
            pltpu.make_async_remote_copy(
                src_ref=pieces.at[p % n_cross], dst_ref=recv_b.at[me_b],
                send_sem=send_b.at[p], recv_sem=got_b.at[me_b], device_id=peer_b(p), device_id_type=MESH,
            ).start()
        return carry

    def wait_loop_b(p, carry):
        @pl.when(p != me_b)
        def _():
            pltpu.make_async_remote_copy(
                src_ref=pieces.at[p % n_cross], dst_ref=recv_b.at[p],
                send_sem=send_b.at[p], recv_sem=got_b.at[p], device_id=peer_b(p), device_id_type=MESH,
            ).wait()
        return carry

    lax.fori_loop(0, group_b, send_loop_b, 0)
    recv_b[me_b] = pieces[cross]
    lax.fori_loop(0, group_b, wait_loop_b, 0)

    total = recv_b[0]
    for p in range(1, group_b):
        total = total + recv_b[p]
    total_s[...] = total * scale
    for r in range(rank):
        mode_ref[r : r + 1, :] = total_s[r // per_row : r // per_row + 1, (r % per_row) * span : (r % per_row + 1) * span]


def local(density, roll_start, mach_factor, cross_factor):
    rolls_here, bins_here, cross_here = density.shape
    rank = cross_factor.shape[0]
    n_roll = lax.axis_size("roll")
    n_mach = lax.axis_size("mach")
    n_cross = lax.axis_size("cross")
    n_chunks = 4
    n_x = 4 if n_mach % 4 == 0 else n_mach
    pay_rows = 3 * rank * rank // 128
    span = bins_here // n_cross
    scale = rank / (rolls_here * n_roll * cross_here * n_cross)
    roll_factor, mode_two = pl.pallas_call(
        functools.partial(fused_kernel, n_roll, n_cross, scale, n_chunks),
        out_shape=(
            jax.ShapeDtypeStruct(roll_start.shape, jnp.float32),
            jax.ShapeDtypeStruct((rank, span), jnp.float32),
        ),
        in_specs=[pl.BlockSpec(memory_space=pl.ANY)] + [pl.BlockSpec(memory_space=VMEM)] * 3,
        out_specs=[pl.BlockSpec(memory_space=VMEM)] * 2,
        scratch_shapes=[
            VMEM(density.shape, density.dtype),
            pltpu.SemaphoreType.DMA((n_chunks,)),
            VMEM((rolls_here, rank, bins_here), jnp.float32),
            VMEM((3, rank, rank), jnp.float32),
            VMEM((pay_rows, 128), jnp.float32),
            VMEM((n_cross, 16, 128), jnp.float32),
            pltpu.SemaphoreType.DMA((n_cross,)),
            pltpu.SemaphoreType.DMA((n_cross,)),
            VMEM((16, 128), jnp.float32),
            VMEM((n_x, 16, 128), jnp.float32),
            pltpu.SemaphoreType.DMA((n_x,)),
            pltpu.SemaphoreType.DMA((n_x,)),
            VMEM((16, 128), jnp.float32),
            VMEM((n_mach // n_x, 16, 128), jnp.float32),
            pltpu.SemaphoreType.DMA((n_mach // n_x,)),
            pltpu.SemaphoreType.DMA((n_mach // n_x,)),
            VMEM((rank, rank), jnp.float32),
            VMEM((rank, rank), jnp.float32),
            VMEM((rank, rank), jnp.float32),
            VMEM((rank, bins_here), jnp.float32),
            VMEM((n_cross, rank * span // 128, 128), jnp.float32),
            VMEM((n_roll * n_cross, rank * span // 128, 128), jnp.float32),
            pltpu.SemaphoreType.DMA((n_roll * n_cross,)),
            pltpu.SemaphoreType.DMA((n_roll * n_cross,)),
            VMEM((rank * span // 128, 128), jnp.float32),
        ],
        compiler_params=pltpu.CompilerParams(collective_id=0, has_side_effects=True),
    )(density, cross_factor, mach_factor, roll_start)
    return (roll_factor, mode_two)


def solution(mesh):
    in_specs = (P("roll", "mach", "cross"), P(None, "roll"), P(None, "mach"), P(None, "cross"))
    out_specs = (P(None, "roll"), P(None, ("mach", "cross")))
    return jax.shard_map(local, mesh=mesh, in_specs=in_specs, out_specs=out_specs, check_vma=False)
```

```python
import functools

import jax
import jax.numpy as jnp
from jax import lax
from jax.experimental import pallas as pl
from jax.experimental.pallas import tpu as pltpu
from jax.sharding import PartitionSpec as P

MESH = pl.DeviceIdType.MESH
VMEM = pltpu.VMEM


def fused_kernel(n_roll, n_cross, scale, n_chunks, dens_hbm, cross_ref, mach_ref, start_ref, rf_ref, mode_ref,
                 dens_v, dens_sem, part_ref, local_s, pay_ref,
                 recv_1, send_1, got_1, pay_2, recv_2, send_2, got_2, gm_s, mt_s, gc_s, term_s, pieces, recv_b, send_b, got_b):
    roll = lax.axis_index("roll")
    mach = lax.axis_index("mach")
    cross = lax.axis_index("cross")
    n_mach = recv_2.shape[0]
    group_b = recv_b.shape[0]
    me_b = roll * n_cross + cross
    rank = rf_ref.shape[0]

    def peer_c(p):
        return (roll, mach, p)

    def peer_m(p):
        return (roll, p, cross)

    def peer_b(p):
        return (p // n_cross, mach, p % n_cross)

    rolls_here = dens_v.shape[0]
    chunk = rolls_here // n_chunks
    loads = [
        pltpu.make_async_copy(dens_hbm.at[pl.ds(k * chunk, chunk)], dens_v.at[pl.ds(k * chunk, chunk)], dens_sem.at[k])
        for k in range(n_chunks)
    ]
    for load in loads:
        load.start()

    barrier = pltpu.get_barrier_semaphore()

    def greet_m(p, carry):
        @pl.when(p != mach)
        def _():
            pl.semaphore_signal(barrier, inc=1, device_id=peer_m(p), device_id_type=MESH)
        return carry

    def greet_b(p, carry):
        @pl.when(p // n_cross != roll)
        def _():
            pl.semaphore_signal(barrier, inc=1, device_id=peer_b(p), device_id_type=MESH)
        return carry

    lax.fori_loop(0, n_mach, greet_m, 0)
    for p in range(n_cross):
        @pl.when(p != cross)
        def _():
            pl.semaphore_signal(barrier, inc=1, device_id=peer_c(p), device_id_type=MESH)
    lax.fori_loop(0, group_b, greet_b, 0)

    nt = (((1,), (1,)), ((), ()))
    cross_f = cross_ref[...]
    mach_f = mach_ref[...]
    mach_w = mach_f.astype(jnp.float32)
    local_s[0] = lax.dot_general(mach_f, mach_f, nt, preferred_element_type=jnp.float32)
    local_s[2] = lax.dot_general(cross_f, cross_f, nt, preferred_element_type=jnp.float32)
    lane = lax.broadcasted_iota(jnp.int32, (rank, rolls_here), 1)
    terms_local = jnp.zeros((rank, rolls_here), jnp.float32)
    for k in range(n_chunks):
        loads[k].wait()
        for i in range(k * chunk, (k + 1) * chunk):
            value = lax.dot_general(cross_f, dens_v[i], nt, preferred_element_type=jnp.float32)
            part_ref[i] = value
            column = jnp.sum(value * mach_w, axis=1, keepdims=True)
            terms_local = jnp.where(lane == i, column, terms_local)
    local_s[1] = terms_local
    for k in range(3):
        for g in range(4):
            pay_ref[8 * k : 8 * k + 8, g * 32 : (g + 1) * 32] = local_s[k, pl.ds(g, 8, stride=4), :]

    pl.semaphore_wait(barrier, n_mach - 1 + group_b - 1)

    def stage_1(p):
        return pltpu.make_async_remote_copy(
            src_ref=pay_ref.at[pl.ds(8, 16)], dst_ref=recv_1.at[cross], send_sem=send_1.at[p],
            recv_sem=got_1.at[cross], device_id=peer_c(p), device_id_type=MESH)

    def stage_1_in(p):
        return pltpu.make_async_remote_copy(
            src_ref=pay_ref.at[pl.ds(8, 16)], dst_ref=recv_1.at[p], send_sem=send_1.at[p],
            recv_sem=got_1.at[p], device_id=peer_c(p), device_id_type=MESH)

    for p in range(n_cross):
        @pl.when(p != cross)
        def _():
            stage_1(p).start()
    recv_1[cross] = pay_ref[8:24, :]
    for p in range(n_cross):
        @pl.when(p != cross)
        def _():
            stage_1_in(p).wait()
    terms = recv_1[0, 0:8, :]
    gc = recv_1[0, 8:16, :]
    for p in range(1, n_cross):
        terms = terms + recv_1[p, 0:8, :]
        gc = gc + recv_1[p, 8:16, :]

    pay_2[0:8, :] = pay_ref[0:8, :]
    pay_2[8:16, :] = terms

    def send_loop_2(p, carry):
        @pl.when(p != mach)
        def _():
            pltpu.make_async_remote_copy(
                src_ref=pay_2, dst_ref=recv_2.at[mach], send_sem=send_2.at[p], recv_sem=got_2.at[mach],
                device_id=peer_m(p), device_id_type=MESH).start()
        return carry

    def wait_loop_2(p, carry):
        @pl.when(p != mach)
        def _():
            pltpu.make_async_remote_copy(
                src_ref=pay_2, dst_ref=recv_2.at[p], send_sem=send_2.at[p], recv_sem=got_2.at[p],
                device_id=peer_m(p), device_id_type=MESH).wait()
        return carry

    lax.fori_loop(0, n_mach, send_loop_2, 0)
    recv_2[mach] = pay_2[...]
    lax.fori_loop(0, n_mach, wait_loop_2, 0)
    gm = recv_2[0, 0:8, :]
    terms = recv_2[0, 8:16, :]
    for p in range(1, n_mach):
        gm = gm + recv_2[p, 0:8, :]
        terms = terms + recv_2[p, 8:16, :]
    for g in range(4):
        lanes = slice(g * 32, (g + 1) * 32)
        gm_s[pl.ds(g, 8, stride=4), :] = gm[:, lanes]
        mt_s[pl.ds(g, 8, stride=4), :] = terms[:, lanes]
        gc_s[pl.ds(g, 8, stride=4), :] = gc[:, lanes]

    gram = gm_s[...] * gc_s[...]
    target = mt_s[...]
    rows = start_ref[...]
    mixed = gram[:, 0:1] * rows[0:1, :]
    for s_ in range(1, rank):
        mixed = mixed + gram[:, s_ : s_ + 1] * rows[s_ : s_ + 1, :]
    for r in range(rank):
        current = rows[r : r + 1, :]
        updated = jnp.maximum(current + (target[r : r + 1, :] - mixed[r : r + 1, :]) / gram[r : r + 1, r : r + 1], 0.0)
        rf_ref[r : r + 1, :] = updated
        mixed = mixed + gram[:, r : r + 1] * (updated - current)

    factor = rf_ref[...]
    term = part_ref[0] * factor[:, 0:1]
    for i in range(1, part_ref.shape[0]):
        term = term + part_ref[i] * factor[:, i : i + 1]
    term_s[...] = term
    span = term_s.shape[1] // n_cross
    per_row = 128 // span
    for c in range(n_cross):
        for r in range(rank):
            pieces[c, r // per_row : r // per_row + 1, (r % per_row) * span : (r % per_row + 1) * span] = (
                term_s[r : r + 1, c * span : (c + 1) * span])

    def send_loop_b(p, carry):
        @pl.when(p != me_b)
        def _():
            pltpu.make_async_remote_copy(
                src_ref=pieces.at[p % n_cross], dst_ref=recv_b.at[me_b],
                send_sem=send_b.at[p], recv_sem=got_b.at[me_b], device_id=peer_b(p), device_id_type=MESH,
            ).start()
        return carry

    def wait_loop_b(p, carry):
        @pl.when(p != me_b)
        def _():
            pltpu.make_async_remote_copy(
                src_ref=pieces.at[p % n_cross], dst_ref=recv_b.at[p],
                send_sem=send_b.at[p], recv_sem=got_b.at[p], device_id=peer_b(p), device_id_type=MESH,
            ).wait()
        return carry

    lax.fori_loop(0, group_b, send_loop_b, 0)
    recv_b[me_b] = pieces[cross]
    lax.fori_loop(0, group_b, wait_loop_b, 0)

    total = recv_b[0]
    for p in range(1, group_b):
        total = total + recv_b[p]
    mode_ref[...] = total * scale


def finish_kernel(rf_ref, total_ref, rf_out, mode_out):
    rf_out[...] = rf_ref[...]
    span = mode_out.shape[1]
    per_row = 128 // span
    for r in range(mode_out.shape[0]):
        mode_out[r : r + 1, :] = total_ref[r // per_row : r // per_row + 1, (r % per_row) * span : (r % per_row + 1) * span]


def local(density, roll_start, mach_factor, cross_factor):
    rolls_here, bins_here, cross_here = density.shape
    rank = cross_factor.shape[0]
    n_roll = lax.axis_size("roll")
    n_mach = lax.axis_size("mach")
    n_cross = lax.axis_size("cross")
    n_chunks = 4
    pay_rows = 3 * rank * rank // 128
    span = bins_here // n_cross
    scale = rank / (rolls_here * n_roll * cross_here * n_cross)
    roll_factor, mode_two = pl.pallas_call(
        functools.partial(fused_kernel, n_roll, n_cross, scale, n_chunks),
        out_shape=(
            jax.ShapeDtypeStruct(roll_start.shape, jnp.float32),
            jax.ShapeDtypeStruct((rank * span // 128, 128), jnp.float32),
        ),
        in_specs=[pl.BlockSpec(memory_space=pl.ANY)] + [pl.BlockSpec(memory_space=VMEM)] * 3,
        out_specs=[pl.BlockSpec(memory_space=VMEM)] * 2,
        scratch_shapes=[
            VMEM(density.shape, density.dtype),
            pltpu.SemaphoreType.DMA((n_chunks,)),
            VMEM((rolls_here, rank, bins_here), jnp.float32),
            VMEM((3, rank, rank), jnp.float32),
            VMEM((pay_rows, 128), jnp.float32),
            VMEM((n_cross, 16, 128), jnp.float32),
            pltpu.SemaphoreType.DMA((n_cross,)),
            pltpu.SemaphoreType.DMA((n_cross,)),
            VMEM((16, 128), jnp.float32),
            VMEM((n_mach, 16, 128), jnp.float32),
            pltpu.SemaphoreType.DMA((n_mach,)),
            pltpu.SemaphoreType.DMA((n_mach,)),
            VMEM((rank, rank), jnp.float32),
            VMEM((rank, rank), jnp.float32),
            VMEM((rank, rank), jnp.float32),
            VMEM((rank, bins_here), jnp.float32),
            VMEM((n_cross, rank * span // 128, 128), jnp.float32),
            VMEM((n_roll * n_cross, rank * span // 128, 128), jnp.float32),
            pltpu.SemaphoreType.DMA((n_roll * n_cross,)),
            pltpu.SemaphoreType.DMA((n_roll * n_cross,)),
        ],
        compiler_params=pltpu.CompilerParams(collective_id=0, has_side_effects=True),
    )(density, cross_factor, mach_factor, roll_start)
    return pl.pallas_call(
        finish_kernel,
        out_shape=(
            jax.ShapeDtypeStruct(roll_start.shape, jnp.float32),
            jax.ShapeDtypeStruct((rank, span), jnp.float32),
        ),
        in_specs=[pl.BlockSpec(memory_space=VMEM)] * 2,
        out_specs=[pl.BlockSpec(memory_space=VMEM)] * 2,
    )(roll_factor, mode_two)


def solution(mesh):
    in_specs = (P("roll", "mach", "cross"), P(None, "roll"), P(None, "mach"), P(None, "cross"))
    out_specs = (P(None, "roll"), P(None, ("mach", "cross")))
    return jax.shard_map(local, mesh=mesh, in_specs=in_specs, out_specs=out_specs, check_vma=False)
```

```python
import functools

import jax
import jax.numpy as jnp
from jax import lax
from jax.experimental import pallas as pl
from jax.experimental.pallas import tpu as pltpu
from jax.sharding import PartitionSpec as P

MESH = pl.DeviceIdType.MESH
VMEM = pltpu.VMEM


def fused_kernel(n_roll, n_cross, scale, n_chunks, dens_hbm, cross_ref, mach_ref, start_ref, rf_ref, mode_ref,
                 dens_v, dens_sem, part_ref, local_s, pay_ref,
                 recv_1, send_1, got_1, pay_2, recv_2, send_2, got_2, gm_s, mt_s, gc_s, term_s, pieces, recv_b, send_b, got_b):
    roll = lax.axis_index("roll")
    mach = lax.axis_index("mach")
    cross = lax.axis_index("cross")
    n_mach = recv_2.shape[0]
    group_b = recv_b.shape[0]
    me_b = roll * n_cross + cross
    rank = rf_ref.shape[0]

    def peer_c(p):
        return (roll, mach, p)

    def peer_m(p):
        return (roll, p, cross)

    def peer_b(p):
        return (p // n_cross, mach, p % n_cross)

    rolls_here = dens_v.shape[0]
    chunk = rolls_here // n_chunks
    loads = [
        pltpu.make_async_copy(dens_hbm.at[pl.ds(k * chunk, chunk)], dens_v.at[pl.ds(k * chunk, chunk)], dens_sem.at[k])
        for k in range(n_chunks)
    ]
    for load in loads:
        load.start()

    barrier = pltpu.get_barrier_semaphore()

    def greet_m(p, carry):
        @pl.when(p != mach)
        def _():
            pl.semaphore_signal(barrier, inc=1, device_id=peer_m(p), device_id_type=MESH)
        return carry

    def greet_b(p, carry):
        @pl.when(p // n_cross != roll)
        def _():
            pl.semaphore_signal(barrier, inc=1, device_id=peer_b(p), device_id_type=MESH)
        return carry

    for p in range(n_mach):
        greet_m(p, 0)
    for p in range(n_cross):
        @pl.when(p != cross)
        def _():
            pl.semaphore_signal(barrier, inc=1, device_id=peer_c(p), device_id_type=MESH)
    for p in range(group_b):
        greet_b(p, 0)

    nt = (((1,), (1,)), ((), ()))
    cross_f = cross_ref[...]
    mach_f = mach_ref[...]
    mach_w = mach_f.astype(jnp.float32)
    local_s[0] = lax.dot_general(mach_f, mach_f, nt, preferred_element_type=jnp.float32)
    local_s[2] = lax.dot_general(cross_f, cross_f, nt, preferred_element_type=jnp.float32)
    lane = lax.broadcasted_iota(jnp.int32, (rank, rolls_here), 1)
    terms_local = jnp.zeros((rank, rolls_here), jnp.float32)
    for k in range(n_chunks):
        loads[k].wait()
        for i in range(k * chunk, (k + 1) * chunk):
            value = lax.dot_general(cross_f, dens_v[i], nt, preferred_element_type=jnp.float32)
            part_ref[i] = value
            column = jnp.sum(value * mach_w, axis=1, keepdims=True)
            terms_local = jnp.where(lane == i, column, terms_local)
    local_s[1] = terms_local
    for k in range(3):
        for g in range(4):
            pay_ref[8 * k : 8 * k + 8, g * 32 : (g + 1) * 32] = local_s[k, pl.ds(g, 8, stride=4), :]

    pl.semaphore_wait(barrier, n_mach - 1 + group_b - 1)

    def stage_1(p):
        return pltpu.make_async_remote_copy(
            src_ref=pay_ref.at[pl.ds(8, 16)], dst_ref=recv_1.at[cross], send_sem=send_1.at[p],
            recv_sem=got_1.at[cross], device_id=peer_c(p), device_id_type=MESH)

    def stage_1_in(p):
        return pltpu.make_async_remote_copy(
            src_ref=pay_ref.at[pl.ds(8, 16)], dst_ref=recv_1.at[p], send_sem=send_1.at[p],
            recv_sem=got_1.at[p], device_id=peer_c(p), device_id_type=MESH)

    for p in range(n_cross):
        @pl.when(p != cross)
        def _():
            stage_1(p).start()
    recv_1[cross] = pay_ref[8:24, :]
    for p in range(n_cross):
        @pl.when(p != cross)
        def _():
            stage_1_in(p).wait()
    terms = recv_1[0, 0:8, :]
    gc = recv_1[0, 8:16, :]
    for p in range(1, n_cross):
        terms = terms + recv_1[p, 0:8, :]
        gc = gc + recv_1[p, 8:16, :]

    pay_2[0:8, :] = pay_ref[0:8, :]
    pay_2[8:16, :] = terms

    def send_loop_2(p, carry):
        @pl.when(p != mach)
        def _():
            pltpu.make_async_remote_copy(
                src_ref=pay_2, dst_ref=recv_2.at[mach], send_sem=send_2.at[p], recv_sem=got_2.at[mach],
                device_id=peer_m(p), device_id_type=MESH).start()
        return carry

    def wait_loop_2(p, carry):
        @pl.when(p != mach)
        def _():
            pltpu.make_async_remote_copy(
                src_ref=pay_2, dst_ref=recv_2.at[p], send_sem=send_2.at[p], recv_sem=got_2.at[p],
                device_id=peer_m(p), device_id_type=MESH).wait()
        return carry

    for p in range(n_mach):
        send_loop_2(p, 0)
    recv_2[mach] = pay_2[...]
    for p in range(n_mach):
        wait_loop_2(p, 0)
    gm = recv_2[0, 0:8, :]
    terms = recv_2[0, 8:16, :]
    for p in range(1, n_mach):
        gm = gm + recv_2[p, 0:8, :]
        terms = terms + recv_2[p, 8:16, :]
    for g in range(4):
        lanes = slice(g * 32, (g + 1) * 32)
        gm_s[pl.ds(g, 8, stride=4), :] = gm[:, lanes]
        mt_s[pl.ds(g, 8, stride=4), :] = terms[:, lanes]
        gc_s[pl.ds(g, 8, stride=4), :] = gc[:, lanes]

    gram = gm_s[...] * gc_s[...]
    target = mt_s[...]
    rows = start_ref[...]
    mixed = gram[:, 0:1] * rows[0:1, :]
    for s_ in range(1, rank):
        mixed = mixed + gram[:, s_ : s_ + 1] * rows[s_ : s_ + 1, :]
    for r in range(rank):
        current = rows[r : r + 1, :]
        updated = jnp.maximum(current + (target[r : r + 1, :] - mixed[r : r + 1, :]) / gram[r : r + 1, r : r + 1], 0.0)
        rf_ref[r : r + 1, :] = updated
        mixed = mixed + gram[:, r : r + 1] * (updated - current)

    factor = rf_ref[...]
    bins_here_k = term_s.shape[0] * 128
    term = part_ref[0] * factor[:, 0:1]
    for i in range(1, part_ref.shape[0]):
        term = term + part_ref[i] * factor[:, i : i + 1]
    for t in range(term_s.shape[0]):
        term_s[t] = term[:, t * 128 : (t + 1) * 128]
    span = bins_here_k // n_cross
    per_row = 128 // span
    for c in range(n_cross):
        lo = (c * span) % 128
        for h in range(per_row):
            rows = term_s[(c * span) // 128, pl.ds(h, rank // per_row, stride=per_row), :]
            pieces[c, :, h * span : (h + 1) * span] = rows[:, lo : lo + span]

    def send_loop_b(p, carry):
        @pl.when(p != me_b)
        def _():
            pltpu.make_async_remote_copy(
                src_ref=pieces.at[p % n_cross], dst_ref=recv_b.at[me_b],
                send_sem=send_b.at[p], recv_sem=got_b.at[me_b], device_id=peer_b(p), device_id_type=MESH,
            ).start()
        return carry

    def wait_loop_b(p, carry):
        @pl.when(p != me_b)
        def _():
            pltpu.make_async_remote_copy(
                src_ref=pieces.at[p % n_cross], dst_ref=recv_b.at[p],
                send_sem=send_b.at[p], recv_sem=got_b.at[p], device_id=peer_b(p), device_id_type=MESH,
            ).wait()
        return carry

    for p in range(group_b):
        send_loop_b(p, 0)
    recv_b[me_b] = pieces[cross]
    for p in range(group_b):
        wait_loop_b(p, 0)

    total = recv_b[0]
    for p in range(1, group_b):
        total = total + recv_b[p]
    mode_ref[...] = total * scale


def finish_kernel(rf_ref, total_ref, rf_out, mode_out):
    rf_out[...] = rf_ref[...]
    span = mode_out.shape[1]
    per_row = 128 // span
    for r in range(mode_out.shape[0]):
        mode_out[r : r + 1, :] = total_ref[r // per_row : r // per_row + 1, (r % per_row) * span : (r % per_row + 1) * span]


def local(density, roll_start, mach_factor, cross_factor):
    rolls_here, bins_here, cross_here = density.shape
    rank = cross_factor.shape[0]
    n_roll = lax.axis_size("roll")
    n_mach = lax.axis_size("mach")
    n_cross = lax.axis_size("cross")
    n_chunks = 4
    pay_rows = 3 * rank * rank // 128
    span = bins_here // n_cross
    scale = rank / (rolls_here * n_roll * cross_here * n_cross)
    roll_factor, mode_two = pl.pallas_call(
        functools.partial(fused_kernel, n_roll, n_cross, scale, n_chunks),
        out_shape=(
            jax.ShapeDtypeStruct(roll_start.shape, jnp.float32),
            jax.ShapeDtypeStruct((rank * span // 128, 128), jnp.float32),
        ),
        in_specs=[pl.BlockSpec(memory_space=pl.ANY)] + [pl.BlockSpec(memory_space=VMEM)] * 3,
        out_specs=[pl.BlockSpec(memory_space=VMEM)] * 2,
        scratch_shapes=[
            VMEM(density.shape, density.dtype),
            pltpu.SemaphoreType.DMA((n_chunks,)),
            VMEM((rolls_here, rank, bins_here), jnp.float32),
            VMEM((3, rank, rank), jnp.float32),
            VMEM((pay_rows, 128), jnp.float32),
            VMEM((n_cross, 16, 128), jnp.float32),
            pltpu.SemaphoreType.DMA((n_cross,)),
            pltpu.SemaphoreType.DMA((n_cross,)),
            VMEM((16, 128), jnp.float32),
            VMEM((n_mach, 16, 128), jnp.float32),
            pltpu.SemaphoreType.DMA((n_mach,)),
            pltpu.SemaphoreType.DMA((n_mach,)),
            VMEM((rank, rank), jnp.float32),
            VMEM((rank, rank), jnp.float32),
            VMEM((rank, rank), jnp.float32),
            VMEM((bins_here // 128, rank, 128), jnp.float32),
            VMEM((n_cross, rank * span // 128, 128), jnp.float32),
            VMEM((n_roll * n_cross, rank * span // 128, 128), jnp.float32),
            pltpu.SemaphoreType.DMA((n_roll * n_cross,)),
            pltpu.SemaphoreType.DMA((n_roll * n_cross,)),
        ],
        compiler_params=pltpu.CompilerParams(collective_id=0, has_side_effects=True),
    )(density, cross_factor, mach_factor, roll_start)
    return pl.pallas_call(
        finish_kernel,
        out_shape=(
            jax.ShapeDtypeStruct(roll_start.shape, jnp.float32),
            jax.ShapeDtypeStruct((rank, span), jnp.float32),
        ),
        in_specs=[pl.BlockSpec(memory_space=VMEM)] * 2,
        out_specs=[pl.BlockSpec(memory_space=VMEM)] * 2,
    )(roll_factor, mode_two)


def solution(mesh):
    in_specs = (P("roll", "mach", "cross"), P(None, "roll"), P(None, "mach"), P(None, "cross"))
    out_specs = (P(None, "roll"), P(None, ("mach", "cross")))
    return jax.shard_map(local, mesh=mesh, in_specs=in_specs, out_specs=out_specs, check_vma=False)
```

```python
import functools

import jax
import jax.numpy as jnp
from jax import lax
from jax.experimental import pallas as pl
from jax.experimental.pallas import tpu as pltpu
from jax.sharding import PartitionSpec as P

MESH = pl.DeviceIdType.MESH
VMEM = pltpu.VMEM


def far_first(n):
    return sorted(range(1, n), key=lambda d: -min(d, n - d))


def fused_kernel(n_roll, n_cross, scale, n_chunks, dens_hbm, cross_ref, mach_ref, start_ref, rf_ref, mode_ref,
                 dens_v, dens_sem, part_ref, local_s, pay_ref,
                 recv_1, send_1, got_1, pay_2, recv_2, send_2, got_2, gm_s, mt_s, gc_s, term_s, pieces, recv_b, send_b, got_b):
    roll = lax.axis_index("roll")
    mach = lax.axis_index("mach")
    cross = lax.axis_index("cross")
    n_mach = recv_2.shape[0]
    group_b = recv_b.shape[0]
    me_b = roll * n_cross + cross
    rank = rf_ref.shape[0]

    def peer_c(p):
        return (roll, mach, p)

    def peer_m(p):
        return (roll, p, cross)

    def peer_b(p):
        return (p // n_cross, mach, p % n_cross)

    rolls_here = dens_v.shape[0]
    chunk = rolls_here // n_chunks
    loads = [
        pltpu.make_async_copy(dens_hbm.at[pl.ds(k * chunk, chunk)], dens_v.at[pl.ds(k * chunk, chunk)], dens_sem.at[k])
        for k in range(n_chunks)
    ]
    for load in loads:
        load.start()

    barrier = pltpu.get_barrier_semaphore()

    def greet_m(p, carry):
        @pl.when(p != mach)
        def _():
            pl.semaphore_signal(barrier, inc=1, device_id=peer_m(p), device_id_type=MESH)
        return carry

    def greet_b(p, carry):
        @pl.when(p // n_cross != roll)
        def _():
            pl.semaphore_signal(barrier, inc=1, device_id=peer_b(p), device_id_type=MESH)
        return carry

    for p in range(n_mach):
        greet_m(p, 0)
    for p in range(n_cross):
        @pl.when(p != cross)
        def _():
            pl.semaphore_signal(barrier, inc=1, device_id=peer_c(p), device_id_type=MESH)
    for p in range(group_b):
        greet_b(p, 0)

    nt = (((1,), (1,)), ((), ()))
    cross_f = cross_ref[...]
    mach_f = mach_ref[...]
    mach_w = mach_f.astype(jnp.float32)
    local_s[0] = lax.dot_general(mach_f, mach_f, nt, preferred_element_type=jnp.float32)
    local_s[2] = lax.dot_general(cross_f, cross_f, nt, preferred_element_type=jnp.float32)
    lane = lax.broadcasted_iota(jnp.int32, (rank, rolls_here), 1)
    terms_local = jnp.zeros((rank, rolls_here), jnp.float32)
    for k in range(n_chunks):
        loads[k].wait()
        for i in range(k * chunk, (k + 1) * chunk):
            value = lax.dot_general(cross_f, dens_v[i], nt, preferred_element_type=jnp.float32)
            part_ref[i] = value
            column = jnp.sum(value * mach_w, axis=1, keepdims=True)
            terms_local = jnp.where(lane == i, column, terms_local)
    local_s[1] = terms_local
    for k in range(3):
        for g in range(4):
            pay_ref[8 * k : 8 * k + 8, g * 32 : (g + 1) * 32] = local_s[k, pl.ds(g, 8, stride=4), :]

    pl.semaphore_wait(barrier, n_mach - 1 + group_b - 1)

    def stage_1(p):
        return pltpu.make_async_remote_copy(
            src_ref=pay_ref.at[pl.ds(8, 16)], dst_ref=recv_1.at[cross], send_sem=send_1.at[p],
            recv_sem=got_1.at[cross], device_id=peer_c(p), device_id_type=MESH)

    def stage_1_in(p):
        return pltpu.make_async_remote_copy(
            src_ref=pay_ref.at[pl.ds(8, 16)], dst_ref=recv_1.at[p], send_sem=send_1.at[p],
            recv_sem=got_1.at[p], device_id=peer_c(p), device_id_type=MESH)

    for dc in far_first(n_cross):
        stage_1((cross + dc) % n_cross).start()
    recv_1[cross] = pay_ref[8:24, :]
    for p in range(n_cross):
        @pl.when(p != cross)
        def _():
            stage_1_in(p).wait()
    terms = recv_1[0, 0:8, :]
    gc = recv_1[0, 8:16, :]
    for p in range(1, n_cross):
        terms = terms + recv_1[p, 0:8, :]
        gc = gc + recv_1[p, 8:16, :]

    pay_2[0:8, :] = pay_ref[0:8, :]
    pay_2[8:16, :] = terms

    def wait_loop_2(p, carry):
        @pl.when(p != mach)
        def _():
            pltpu.make_async_remote_copy(
                src_ref=pay_2, dst_ref=recv_2.at[p], send_sem=send_2.at[p], recv_sem=got_2.at[p],
                device_id=peer_m(p), device_id_type=MESH).wait()
        return carry

    n_x = 4 if n_mach % 4 == 0 else n_mach
    n_y = n_mach // n_x
    offsets = [(dy, dx) for dy in range(n_y) for dx in range(n_x) if (dy, dx) != (0, 0)]
    offsets.sort(key=lambda o: -(min(o[0], n_y - o[0]) + min(o[1], n_x - o[1])))
    for dy, dx in offsets:
        p = ((mach // n_x + dy) % n_y) * n_x + (mach % n_x + dx) % n_x
        pltpu.make_async_remote_copy(
            src_ref=pay_2, dst_ref=recv_2.at[mach], send_sem=send_2.at[p], recv_sem=got_2.at[mach],
            device_id=peer_m(p), device_id_type=MESH).start()
    recv_2[mach] = pay_2[...]
    for p in range(n_mach):
        wait_loop_2(p, 0)
    gm = recv_2[0, 0:8, :]
    terms = recv_2[0, 8:16, :]
    for p in range(1, n_mach):
        gm = gm + recv_2[p, 0:8, :]
        terms = terms + recv_2[p, 8:16, :]
    for g in range(4):
        lanes = slice(g * 32, (g + 1) * 32)
        gm_s[pl.ds(g, 8, stride=4), :] = gm[:, lanes]
        mt_s[pl.ds(g, 8, stride=4), :] = terms[:, lanes]
        gc_s[pl.ds(g, 8, stride=4), :] = gc[:, lanes]

    gram = gm_s[...] * gc_s[...]
    target = mt_s[...]
    rows = start_ref[...]
    mixed = gram[:, 0:1] * rows[0:1, :]
    for s_ in range(1, rank):
        mixed = mixed + gram[:, s_ : s_ + 1] * rows[s_ : s_ + 1, :]
    inverse = 1.0 / gram
    for r in range(rank):
        current = rows[r : r + 1, :]
        updated = jnp.maximum(current + (target[r : r + 1, :] - mixed[r : r + 1, :]) * inverse[r : r + 1, r : r + 1], 0.0)
        rf_ref[r : r + 1, :] = updated
        mixed = mixed + gram[:, r : r + 1] * (updated - current)

    factor = rf_ref[...]
    bins_here_k = term_s.shape[0] * 128
    term = part_ref[0] * factor[:, 0:1]
    for i in range(1, part_ref.shape[0]):
        term = term + part_ref[i] * factor[:, i : i + 1]
    for t in range(term_s.shape[0]):
        term_s[t] = term[:, t * 128 : (t + 1) * 128]
    span = bins_here_k // n_cross
    per_row = 128 // span
    for c in range(n_cross):
        lo = (c * span) % 128
        for h in range(per_row):
            rows = term_s[(c * span) // 128, pl.ds(h, rank // per_row, stride=per_row), :]
            pieces[c, :, h * span : (h + 1) * span] = rows[:, lo : lo + span]

    def wait_loop_b(p, carry):
        @pl.when(p != me_b)
        def _():
            pltpu.make_async_remote_copy(
                src_ref=pieces.at[p % n_cross], dst_ref=recv_b.at[p],
                send_sem=send_b.at[p], recv_sem=got_b.at[p], device_id=peer_b(p), device_id_type=MESH,
            ).wait()
        return carry

    for dc in [d for d in far_first(n_cross)] + [0]:
        for da in range(n_roll):
            if (da, dc) == (0, 0):
                continue
            p = ((roll + da) % n_roll) * n_cross + (cross + dc) % n_cross
            pltpu.make_async_remote_copy(
                src_ref=pieces.at[(cross + dc) % n_cross], dst_ref=recv_b.at[me_b],
                send_sem=send_b.at[p], recv_sem=got_b.at[me_b], device_id=peer_b(p), device_id_type=MESH,
            ).start()
    recv_b[me_b] = pieces[cross]
    for p in range(group_b):
        wait_loop_b(p, 0)

    total = recv_b[0]
    for p in range(1, group_b):
        total = total + recv_b[p]
    mode_ref[...] = total * scale


def finish_kernel(rf_ref, total_ref, rf_out, mode_out):
    rf_out[...] = rf_ref[...]
    span = mode_out.shape[1]
    per_row = 128 // span
    for r in range(mode_out.shape[0]):
        mode_out[r : r + 1, :] = total_ref[r // per_row : r // per_row + 1, (r % per_row) * span : (r % per_row + 1) * span]


def local(density, roll_start, mach_factor, cross_factor):
    rolls_here, bins_here, cross_here = density.shape
    rank = cross_factor.shape[0]
    n_roll = lax.axis_size("roll")
    n_mach = lax.axis_size("mach")
    n_cross = lax.axis_size("cross")
    n_chunks = 4
    pay_rows = 3 * rank * rank // 128
    span = bins_here // n_cross
    scale = rank / (rolls_here * n_roll * cross_here * n_cross)
    roll_factor, mode_two = pl.pallas_call(
        functools.partial(fused_kernel, n_roll, n_cross, scale, n_chunks),
        out_shape=(
            jax.ShapeDtypeStruct(roll_start.shape, jnp.float32),
            jax.ShapeDtypeStruct((rank * span // 128, 128), jnp.float32),
        ),
        in_specs=[pl.BlockSpec(memory_space=pl.ANY)] + [pl.BlockSpec(memory_space=VMEM)] * 3,
        out_specs=[pl.BlockSpec(memory_space=VMEM)] * 2,
        scratch_shapes=[
            VMEM(density.shape, density.dtype),
            pltpu.SemaphoreType.DMA((n_chunks,)),
            VMEM((rolls_here, rank, bins_here), jnp.float32),
            VMEM((3, rank, rank), jnp.float32),
            VMEM((pay_rows, 128), jnp.float32),
            VMEM((n_cross, 16, 128), jnp.float32),
            pltpu.SemaphoreType.DMA((n_cross,)),
            pltpu.SemaphoreType.DMA((n_cross,)),
            VMEM((16, 128), jnp.float32),
            VMEM((n_mach, 16, 128), jnp.float32),
            pltpu.SemaphoreType.DMA((n_mach,)),
            pltpu.SemaphoreType.DMA((n_mach,)),
            VMEM((rank, rank), jnp.float32),
            VMEM((rank, rank), jnp.float32),
            VMEM((rank, rank), jnp.float32),
            VMEM((bins_here // 128, rank, 128), jnp.float32),
            VMEM((n_cross, rank * span // 128, 128), jnp.float32),
            VMEM((n_roll * n_cross, rank * span // 128, 128), jnp.float32),
            pltpu.SemaphoreType.DMA((n_roll * n_cross,)),
            pltpu.SemaphoreType.DMA((n_roll * n_cross,)),
        ],
        compiler_params=pltpu.CompilerParams(collective_id=0, has_side_effects=True),
    )(density, cross_factor, mach_factor, roll_start)
    return pl.pallas_call(
        finish_kernel,
        out_shape=(
            jax.ShapeDtypeStruct(roll_start.shape, jnp.float32),
            jax.ShapeDtypeStruct((rank, span), jnp.float32),
        ),
        in_specs=[pl.BlockSpec(memory_space=VMEM)] * 2,
        out_specs=[pl.BlockSpec(memory_space=VMEM)] * 2,
    )(roll_factor, mode_two)


def solution(mesh):
    in_specs = (P("roll", "mach", "cross"), P(None, "roll"), P(None, "mach"), P(None, "cross"))
    out_specs = (P(None, "roll"), P(None, ("mach", "cross")))
    return jax.shard_map(local, mesh=mesh, in_specs=in_specs, out_specs=out_specs, check_vma=False)
```

```python
import functools

import jax
import jax.numpy as jnp
from jax import lax
from jax.experimental import pallas as pl
from jax.experimental.pallas import tpu as pltpu
from jax.sharding import PartitionSpec as P

MESH = pl.DeviceIdType.MESH
VMEM = pltpu.VMEM


def fused_kernel(n_roll, n_cross, scale, n_chunks, dens_hbm, cross_ref, mach_ref, start_ref, rf_ref, mode_ref,
                 dens_v, dens_sem, part_ref, local_s, pay_ref,
                 recv_1, send_1, got_1, pay_2, recv_2, send_2, got_2, gm_s, mt_s, gc_s, term_s, pieces, recv_b, send_b, got_b):
    roll = lax.axis_index("roll")
    mach = lax.axis_index("mach")
    cross = lax.axis_index("cross")
    n_mach = recv_2.shape[0]
    group_b = recv_b.shape[0]
    me_b = roll * n_cross + cross
    rank = rf_ref.shape[0]

    def peer_c(p):
        return (roll, mach, p)

    def peer_m(p):
        return (roll, p, cross)

    def peer_b(p):
        return (p // n_cross, mach, p % n_cross)

    rolls_here = dens_v.shape[0]
    chunk = rolls_here // n_chunks
    loads = [
        pltpu.make_async_copy(dens_hbm.at[pl.ds(k * chunk, chunk)], dens_v.at[pl.ds(k * chunk, chunk)], dens_sem.at[k])
        for k in range(n_chunks)
    ]
    for load in loads:
        load.start()

    barrier = pltpu.get_barrier_semaphore()

    def greet_m(p, carry):
        @pl.when(p != mach)
        def _():
            pl.semaphore_signal(barrier, inc=1, device_id=peer_m(p), device_id_type=MESH)
        return carry

    def greet_b(p, carry):
        @pl.when(p // n_cross != roll)
        def _():
            pl.semaphore_signal(barrier, inc=1, device_id=peer_b(p), device_id_type=MESH)
        return carry

    for p in range(n_mach):
        greet_m(p, 0)
    for p in range(n_cross):
        @pl.when(p != cross)
        def _():
            pl.semaphore_signal(barrier, inc=1, device_id=peer_c(p), device_id_type=MESH)
    for p in range(group_b):
        greet_b(p, 0)

    nt = (((1,), (1,)), ((), ()))
    cross_f = cross_ref[...]
    mach_f = mach_ref[...]
    mach_w = mach_f.astype(jnp.float32)
    local_s[0] = lax.dot_general(mach_f, mach_f, nt, preferred_element_type=jnp.float32)
    local_s[2] = lax.dot_general(cross_f, cross_f, nt, preferred_element_type=jnp.float32)
    lane = lax.broadcasted_iota(jnp.int32, (rank, rolls_here), 1)
    terms_local = jnp.zeros((rank, rolls_here), jnp.float32)
    for k in range(n_chunks):
        loads[k].wait()
        for i in range(k * chunk, (k + 1) * chunk):
            value = lax.dot_general(cross_f, dens_v[i], nt, preferred_element_type=jnp.float32)
            part_ref[i] = value
            column = jnp.sum(value * mach_w, axis=1, keepdims=True)
            terms_local = jnp.where(lane == i, column, terms_local)
    local_s[1] = terms_local
    for k in range(3):
        for g in range(4):
            pay_ref[8 * k : 8 * k + 8, g * 32 : (g + 1) * 32] = local_s[k, pl.ds(g, 8, stride=4), :]

    pl.semaphore_wait(barrier, n_mach - 1 + group_b - 1)

    def stage_1(p):
        return pltpu.make_async_remote_copy(
            src_ref=pay_ref.at[pl.ds(8, 16)], dst_ref=recv_1.at[cross], send_sem=send_1.at[p],
            recv_sem=got_1.at[cross], device_id=peer_c(p), device_id_type=MESH)

    def stage_1_in(p):
        return pltpu.make_async_remote_copy(
            src_ref=pay_ref.at[pl.ds(8, 16)], dst_ref=recv_1.at[p], send_sem=send_1.at[p],
            recv_sem=got_1.at[p], device_id=peer_c(p), device_id_type=MESH)

    for p in range(n_cross):
        @pl.when(p != cross)
        def _():
            stage_1(p).start()
    recv_1[cross] = pay_ref[8:24, :]
    for p in range(n_cross):
        @pl.when(p != cross)
        def _():
            stage_1_in(p).wait()
    terms = recv_1[0, 0:8, :]
    gc = recv_1[0, 8:16, :]
    for p in range(1, n_cross):
        terms = terms + recv_1[p, 0:8, :]
        gc = gc + recv_1[p, 8:16, :]

    pay_2[0:8, :] = pay_ref[0:8, :]
    pay_2[8:16, :] = terms

    def send_loop_2(p, carry):
        @pl.when(p != mach)
        def _():
            pltpu.make_async_remote_copy(
                src_ref=pay_2, dst_ref=recv_2.at[mach], send_sem=send_2.at[p], recv_sem=got_2.at[mach],
                device_id=peer_m(p), device_id_type=MESH).start()
        return carry

    def wait_loop_2(p, carry):
        @pl.when(p != mach)
        def _():
            pltpu.make_async_remote_copy(
                src_ref=pay_2, dst_ref=recv_2.at[p], send_sem=send_2.at[p], recv_sem=got_2.at[p],
                device_id=peer_m(p), device_id_type=MESH).wait()
        return carry

    for p in range(n_mach):
        send_loop_2(p, 0)
    recv_2[mach] = pay_2[...]
    for p in range(n_mach):
        wait_loop_2(p, 0)
    gm = recv_2[0, 0:8, :]
    terms = recv_2[0, 8:16, :]
    for p in range(1, n_mach):
        gm = gm + recv_2[p, 0:8, :]
        terms = terms + recv_2[p, 8:16, :]
    for g in range(4):
        lanes = slice(g * 32, (g + 1) * 32)
        gm_s[pl.ds(g, 8, stride=4), :] = gm[:, lanes]
        mt_s[pl.ds(g, 8, stride=4), :] = terms[:, lanes]
        gc_s[pl.ds(g, 8, stride=4), :] = gc[:, lanes]

    gram = gm_s[...] * gc_s[...]
    target = mt_s[...]
    rows = start_ref[...]
    mixed = gram[:, 0:1] * rows[0:1, :]
    for s_ in range(1, rank):
        mixed = mixed + gram[:, s_ : s_ + 1] * rows[s_ : s_ + 1, :]
    inverse = 1.0 / gram
    for r in range(rank):
        current = rows[r : r + 1, :]
        updated = jnp.maximum(current + (target[r : r + 1, :] - mixed[r : r + 1, :]) * inverse[r : r + 1, r : r + 1], 0.0)
        rf_ref[r : r + 1, :] = updated
        mixed = mixed + gram[:, r : r + 1] * (updated - current)

    factor = rf_ref[...]
    bins_here_k = term_s.shape[0] * 128
    term = part_ref[0] * factor[:, 0:1]
    for i in range(1, part_ref.shape[0]):
        term = term + part_ref[i] * factor[:, i : i + 1]
    for t in range(term_s.shape[0]):
        term_s[t] = term[:, t * 128 : (t + 1) * 128]
    span = bins_here_k // n_cross
    per_row = 128 // span
    for c in range(n_cross):
        lo = (c * span) % 128
        for h in range(per_row):
            rows = term_s[(c * span) // 128, pl.ds(h, rank // per_row, stride=per_row), :]
            pieces[c, :, h * span : (h + 1) * span] = rows[:, lo : lo + span]

    def send_loop_b(p, carry):
        @pl.when(p != me_b)
        def _():
            pltpu.make_async_remote_copy(
                src_ref=pieces.at[p % n_cross], dst_ref=recv_b.at[me_b],
                send_sem=send_b.at[p], recv_sem=got_b.at[me_b], device_id=peer_b(p), device_id_type=MESH,
            ).start()
        return carry

    def wait_loop_b(p, carry):
        @pl.when(p != me_b)
        def _():
            pltpu.make_async_remote_copy(
                src_ref=pieces.at[p % n_cross], dst_ref=recv_b.at[p],
                send_sem=send_b.at[p], recv_sem=got_b.at[p], device_id=peer_b(p), device_id_type=MESH,
            ).wait()
        return carry

    for p in range(group_b):
        send_loop_b(p, 0)
    recv_b[me_b] = pieces[cross]
    for p in range(group_b):
        wait_loop_b(p, 0)

    total = recv_b[0]
    for p in range(1, group_b):
        total = total + recv_b[p]
    mode_ref[...] = total * scale


def finish_kernel(rf_ref, total_ref, rf_out, mode_out):
    rf_out[...] = rf_ref[...]
    span = mode_out.shape[1]
    per_row = 128 // span
    for r in range(mode_out.shape[0]):
        mode_out[r : r + 1, :] = total_ref[r // per_row : r // per_row + 1, (r % per_row) * span : (r % per_row + 1) * span]


def local(density, roll_start, mach_factor, cross_factor):
    rolls_here, bins_here, cross_here = density.shape
    rank = cross_factor.shape[0]
    n_roll = lax.axis_size("roll")
    n_mach = lax.axis_size("mach")
    n_cross = lax.axis_size("cross")
    n_chunks = 4
    pay_rows = 3 * rank * rank // 128
    span = bins_here // n_cross
    scale = rank / (rolls_here * n_roll * cross_here * n_cross)
    roll_factor, mode_two = pl.pallas_call(
        functools.partial(fused_kernel, n_roll, n_cross, scale, n_chunks),
        out_shape=(
            jax.ShapeDtypeStruct(roll_start.shape, jnp.float32),
            jax.ShapeDtypeStruct((rank * span // 128, 128), jnp.float32),
        ),
        in_specs=[pl.BlockSpec(memory_space=pl.ANY)] + [pl.BlockSpec(memory_space=VMEM)] * 3,
        out_specs=[pl.BlockSpec(memory_space=VMEM)] * 2,
        scratch_shapes=[
            VMEM(density.shape, density.dtype),
            pltpu.SemaphoreType.DMA((n_chunks,)),
            VMEM((rolls_here, rank, bins_here), jnp.float32),
            VMEM((3, rank, rank), jnp.float32),
            VMEM((pay_rows, 128), jnp.float32),
            VMEM((n_cross, 16, 128), jnp.float32),
            pltpu.SemaphoreType.DMA((n_cross,)),
            pltpu.SemaphoreType.DMA((n_cross,)),
            VMEM((16, 128), jnp.float32),
            VMEM((n_mach, 16, 128), jnp.float32),
            pltpu.SemaphoreType.DMA((n_mach,)),
            pltpu.SemaphoreType.DMA((n_mach,)),
            VMEM((rank, rank), jnp.float32),
            VMEM((rank, rank), jnp.float32),
            VMEM((rank, rank), jnp.float32),
            VMEM((bins_here // 128, rank, 128), jnp.float32),
            VMEM((n_cross, rank * span // 128, 128), jnp.float32),
            VMEM((n_roll * n_cross, rank * span // 128, 128), jnp.float32),
            pltpu.SemaphoreType.DMA((n_roll * n_cross,)),
            pltpu.SemaphoreType.DMA((n_roll * n_cross,)),
        ],
        compiler_params=pltpu.CompilerParams(collective_id=0, has_side_effects=True),
    )(density, cross_factor, mach_factor, roll_start)
    return pl.pallas_call(
        finish_kernel,
        out_shape=(
            jax.ShapeDtypeStruct(roll_start.shape, jnp.float32),
            jax.ShapeDtypeStruct((rank, span), jnp.float32),
        ),
        in_specs=[pl.BlockSpec(memory_space=VMEM)] * 2,
        out_specs=[pl.BlockSpec(memory_space=VMEM)] * 2,
    )(roll_factor, mode_two)


def solution(mesh):
    in_specs = (P("roll", "mach", "cross"), P(None, "roll"), P(None, "mach"), P(None, "cross"))
    out_specs = (P(None, "roll"), P(None, ("mach", "cross")))
    return jax.shard_map(local, mesh=mesh, in_specs=in_specs, out_specs=out_specs, check_vma=False)
```

```python
import functools

import jax
import jax.numpy as jnp
from jax import lax
from jax.experimental import pallas as pl
from jax.experimental.pallas import tpu as pltpu
from jax.sharding import PartitionSpec as P

MESH = pl.DeviceIdType.MESH
VMEM = pltpu.VMEM


def fused_kernel(n_roll, n_cross, scale, n_chunks, dens_hbm, cross_hbm, mach_hbm, start_hbm, rf_ref, mode_ref,
                 cross_ref, mach_ref, start_ref, small_sem, dens_v, dens_sem, part_ref, local_s, pay_ref,
                 recv_1, send_1, got_1, pay_2, recv_2, send_2, got_2, gm_s, mt_s, gc_s, term_s, pieces, recv_b, send_b, got_b):
    roll = lax.axis_index("roll")
    mach = lax.axis_index("mach")
    cross = lax.axis_index("cross")
    n_mach = recv_2.shape[0]
    group_b = recv_b.shape[0]
    me_b = roll * n_cross + cross
    rank = rf_ref.shape[0]

    def peer_c(p):
        return (roll, mach, p)

    def peer_m(p):
        return (roll, p, cross)

    def peer_b(p):
        return (p // n_cross, mach, p % n_cross)

    rolls_here = dens_v.shape[0]
    chunk = rolls_here // n_chunks
    loads = [
        pltpu.make_async_copy(dens_hbm.at[pl.ds(k * chunk, chunk)], dens_v.at[pl.ds(k * chunk, chunk)], dens_sem.at[k])
        for k in range(n_chunks)
    ]
    small = [
        pltpu.make_async_copy(src, dst, small_sem.at[k])
        for k, (src, dst) in enumerate(((cross_hbm, cross_ref), (mach_hbm, mach_ref), (start_hbm, start_ref)))
    ]
    small[0].start()
    for load in loads:
        load.start()
    small[1].start()
    small[2].start()

    barrier = pltpu.get_barrier_semaphore()

    def greet_m(p, carry):
        @pl.when(p != mach)
        def _():
            pl.semaphore_signal(barrier, inc=1, device_id=peer_m(p), device_id_type=MESH)
        return carry

    def greet_b(p, carry):
        @pl.when(p // n_cross != roll)
        def _():
            pl.semaphore_signal(barrier, inc=1, device_id=peer_b(p), device_id_type=MESH)
        return carry

    for p in range(n_mach):
        greet_m(p, 0)
    for p in range(n_cross):
        @pl.when(p != cross)
        def _():
            pl.semaphore_signal(barrier, inc=1, device_id=peer_c(p), device_id_type=MESH)
    for p in range(group_b):
        greet_b(p, 0)

    nt = (((1,), (1,)), ((), ()))
    small[0].wait()
    small[1].wait()
    cross_f = cross_ref[...]
    mach_f = mach_ref[...]
    mach_w = mach_f.astype(jnp.float32)
    local_s[0] = lax.dot_general(mach_f, mach_f, nt, preferred_element_type=jnp.float32)
    local_s[2] = lax.dot_general(cross_f, cross_f, nt, preferred_element_type=jnp.float32)
    lane = lax.broadcasted_iota(jnp.int32, (rank, rolls_here), 1)
    terms_local = jnp.zeros((rank, rolls_here), jnp.float32)
    for k in range(n_chunks):
        loads[k].wait()
        for i in range(k * chunk, (k + 1) * chunk):
            value = lax.dot_general(cross_f, dens_v[i], nt, preferred_element_type=jnp.float32)
            part_ref[i] = value
            column = jnp.sum(value * mach_w, axis=1, keepdims=True)
            terms_local = jnp.where(lane == i, column, terms_local)
    local_s[1] = terms_local
    for k in range(3):
        for g in range(4):
            pay_ref[8 * k : 8 * k + 8, g * 32 : (g + 1) * 32] = local_s[k, pl.ds(g, 8, stride=4), :]

    pl.semaphore_wait(barrier, n_mach - 1 + group_b - 1)

    def stage_1(p):
        return pltpu.make_async_remote_copy(
            src_ref=pay_ref.at[pl.ds(8, 16)], dst_ref=recv_1.at[cross], send_sem=send_1.at[p],
            recv_sem=got_1.at[cross], device_id=peer_c(p), device_id_type=MESH)

    def stage_1_in(p):
        return pltpu.make_async_remote_copy(
            src_ref=pay_ref.at[pl.ds(8, 16)], dst_ref=recv_1.at[p], send_sem=send_1.at[p],
            recv_sem=got_1.at[p], device_id=peer_c(p), device_id_type=MESH)

    for p in range(n_cross):
        @pl.when(p != cross)
        def _():
            stage_1(p).start()
    recv_1[cross] = pay_ref[8:24, :]
    for p in range(n_cross):
        @pl.when(p != cross)
        def _():
            stage_1_in(p).wait()
    terms = recv_1[0, 0:8, :]
    gc = recv_1[0, 8:16, :]
    for p in range(1, n_cross):
        terms = terms + recv_1[p, 0:8, :]
        gc = gc + recv_1[p, 8:16, :]

    pay_2[0:8, :] = pay_ref[0:8, :]
    pay_2[8:16, :] = terms

    def send_loop_2(p, carry):
        @pl.when(p != mach)
        def _():
            pltpu.make_async_remote_copy(
                src_ref=pay_2, dst_ref=recv_2.at[mach], send_sem=send_2.at[p], recv_sem=got_2.at[mach],
                device_id=peer_m(p), device_id_type=MESH).start()
        return carry

    def wait_loop_2(p, carry):
        @pl.when(p != mach)
        def _():
            pltpu.make_async_remote_copy(
                src_ref=pay_2, dst_ref=recv_2.at[p], send_sem=send_2.at[p], recv_sem=got_2.at[p],
                device_id=peer_m(p), device_id_type=MESH).wait()
        return carry

    for p in range(n_mach):
        send_loop_2(p, 0)
    recv_2[mach] = pay_2[...]
    for p in range(n_mach):
        wait_loop_2(p, 0)
    gm = recv_2[0, 0:8, :]
    terms = recv_2[0, 8:16, :]
    for p in range(1, n_mach):
        gm = gm + recv_2[p, 0:8, :]
        terms = terms + recv_2[p, 8:16, :]
    for g in range(4):
        lanes = slice(g * 32, (g + 1) * 32)
        gm_s[pl.ds(g, 8, stride=4), :] = gm[:, lanes]
        mt_s[pl.ds(g, 8, stride=4), :] = terms[:, lanes]
        gc_s[pl.ds(g, 8, stride=4), :] = gc[:, lanes]

    gram = gm_s[...] * gc_s[...]
    target = mt_s[...]
    small[2].wait()
    rows = start_ref[...]
    mixed = gram[:, 0:1] * rows[0:1, :]
    for s_ in range(1, rank):
        mixed = mixed + gram[:, s_ : s_ + 1] * rows[s_ : s_ + 1, :]
    for r in range(rank):
        current = rows[r : r + 1, :]
        updated = jnp.maximum(current + (target[r : r + 1, :] - mixed[r : r + 1, :]) / gram[r : r + 1, r : r + 1], 0.0)
        rf_ref[r : r + 1, :] = updated
        mixed = mixed + gram[:, r : r + 1] * (updated - current)

    factor = rf_ref[...]
    bins_here_k = term_s.shape[0] * 128
    term = part_ref[0] * factor[:, 0:1]
    for i in range(1, part_ref.shape[0]):
        term = term + part_ref[i] * factor[:, i : i + 1]
    for t in range(term_s.shape[0]):
        term_s[t] = term[:, t * 128 : (t + 1) * 128]
    span = bins_here_k // n_cross
    per_row = 128 // span
    for c in range(n_cross):
        lo = (c * span) % 128
        for h in range(per_row):
            rows = term_s[(c * span) // 128, pl.ds(h, rank // per_row, stride=per_row), :]
            pieces[c, :, h * span : (h + 1) * span] = rows[:, lo : lo + span]

    def send_loop_b(p, carry):
        @pl.when(p != me_b)
        def _():
            pltpu.make_async_remote_copy(
                src_ref=pieces.at[p % n_cross], dst_ref=recv_b.at[me_b],
                send_sem=send_b.at[p], recv_sem=got_b.at[me_b], device_id=peer_b(p), device_id_type=MESH,
            ).start()
        return carry

    def wait_loop_b(p, carry):
        @pl.when(p != me_b)
        def _():
            pltpu.make_async_remote_copy(
                src_ref=pieces.at[p % n_cross], dst_ref=recv_b.at[p],
                send_sem=send_b.at[p], recv_sem=got_b.at[p], device_id=peer_b(p), device_id_type=MESH,
            ).wait()
        return carry

    for p in range(group_b):
        send_loop_b(p, 0)
    recv_b[me_b] = pieces[cross]
    for p in range(group_b):
        wait_loop_b(p, 0)

    total = recv_b[0]
    for p in range(1, group_b):
        total = total + recv_b[p]
    mode_ref[...] = total * scale


def finish_kernel(rf_ref, total_ref, rf_out, mode_out):
    rf_out[...] = rf_ref[...]
    span = mode_out.shape[1]
    per_row = 128 // span
    for r in range(mode_out.shape[0]):
        mode_out[r : r + 1, :] = total_ref[r // per_row : r // per_row + 1, (r % per_row) * span : (r % per_row + 1) * span]


def local(density, roll_start, mach_factor, cross_factor):
    rolls_here, bins_here, cross_here = density.shape
    rank = cross_factor.shape[0]
    n_roll = lax.axis_size("roll")
    n_mach = lax.axis_size("mach")
    n_cross = lax.axis_size("cross")
    n_chunks = 4
    pay_rows = 3 * rank * rank // 128
    span = bins_here // n_cross
    scale = rank / (rolls_here * n_roll * cross_here * n_cross)
    roll_factor, mode_two = pl.pallas_call(
        functools.partial(fused_kernel, n_roll, n_cross, scale, n_chunks),
        out_shape=(
            jax.ShapeDtypeStruct(roll_start.shape, jnp.float32),
            jax.ShapeDtypeStruct((rank * span // 128, 128), jnp.float32),
        ),
        in_specs=[pl.BlockSpec(memory_space=pl.ANY)] * 4,
        out_specs=[pl.BlockSpec(memory_space=VMEM)] * 2,
        scratch_shapes=[
            VMEM(cross_factor.shape, cross_factor.dtype),
            VMEM(mach_factor.shape, mach_factor.dtype),
            VMEM(roll_start.shape, roll_start.dtype),
            pltpu.SemaphoreType.DMA((3,)),
            VMEM(density.shape, density.dtype),
            pltpu.SemaphoreType.DMA((n_chunks,)),
            VMEM((rolls_here, rank, bins_here), jnp.float32),
            VMEM((3, rank, rank), jnp.float32),
            VMEM((pay_rows, 128), jnp.float32),
            VMEM((n_cross, 16, 128), jnp.float32),
            pltpu.SemaphoreType.DMA((n_cross,)),
            pltpu.SemaphoreType.DMA((n_cross,)),
            VMEM((16, 128), jnp.float32),
            VMEM((n_mach, 16, 128), jnp.float32),
            pltpu.SemaphoreType.DMA((n_mach,)),
            pltpu.SemaphoreType.DMA((n_mach,)),
            VMEM((rank, rank), jnp.float32),
            VMEM((rank, rank), jnp.float32),
            VMEM((rank, rank), jnp.float32),
            VMEM((bins_here // 128, rank, 128), jnp.float32),
            VMEM((n_cross, rank * span // 128, 128), jnp.float32),
            VMEM((n_roll * n_cross, rank * span // 128, 128), jnp.float32),
            pltpu.SemaphoreType.DMA((n_roll * n_cross,)),
            pltpu.SemaphoreType.DMA((n_roll * n_cross,)),
        ],
        compiler_params=pltpu.CompilerParams(collective_id=0, has_side_effects=True),
    )(density, cross_factor, mach_factor, roll_start)
    return pl.pallas_call(
        finish_kernel,
        out_shape=(
            jax.ShapeDtypeStruct(roll_start.shape, jnp.float32),
            jax.ShapeDtypeStruct((rank, span), jnp.float32),
        ),
        in_specs=[pl.BlockSpec(memory_space=VMEM)] * 2,
        out_specs=[pl.BlockSpec(memory_space=VMEM)] * 2,
    )(roll_factor, mode_two)


def solution(mesh):
    in_specs = (P("roll", "mach", "cross"), P(None, "roll"), P(None, "mach"), P(None, "cross"))
    out_specs = (P(None, "roll"), P(None, ("mach", "cross")))
    return jax.shard_map(local, mesh=mesh, in_specs=in_specs, out_specs=out_specs, check_vma=False)
```

```python
import functools

import jax
import jax.numpy as jnp
from jax import lax
from jax.experimental import pallas as pl
from jax.experimental.pallas import tpu as pltpu
from jax.sharding import PartitionSpec as P

MESH = pl.DeviceIdType.MESH
VMEM = pltpu.VMEM


def fused_kernel(n_roll, n_cross, scale, n_chunks, dens_hbm, cross_ref, mach_ref, start_ref, rf_ref, mode_ref,
                 dens_v, dens_sem, part_ref, local_s, pay_ref,
                 recv_1, send_1, got_1, pay_2, recv_2, send_2, got_2, gm_s, mt_s, gc_s, term_s, pieces,
                 recv_b1, send_b1, got_b1, core_sum, recv_b2, send_b2, got_b2):
    roll = lax.axis_index("roll")
    mach = lax.axis_index("mach")
    cross = lax.axis_index("cross")
    n_mach = recv_2.shape[0]
    n_core = recv_b1.shape[0]
    n_zl = recv_b2.shape[0] // n_cross
    zl = roll // n_core
    core = roll % n_core
    me_z = zl * n_cross + cross
    rank = rf_ref.shape[0]

    def peer_c(p):
        return (roll, mach, p)

    def peer_m(p):
        return (roll, p, cross)

    def peer_core(q):
        return (zl * n_core + q, mach, cross)

    def peer_z(p):
        return ((p // n_cross) * n_core + core, mach, p % n_cross)

    rolls_here = dens_v.shape[0]
    chunk = rolls_here // n_chunks
    loads = [
        pltpu.make_async_copy(dens_hbm.at[pl.ds(k * chunk, chunk)], dens_v.at[pl.ds(k * chunk, chunk)], dens_sem.at[k])
        for k in range(n_chunks)
    ]
    for load in loads:
        load.start()

    barrier = pltpu.get_barrier_semaphore()

    def greet_m(p, carry):
        @pl.when(p != mach)
        def _():
            pl.semaphore_signal(barrier, inc=1, device_id=peer_m(p), device_id_type=MESH)
        return carry

    def greet_b(p, carry):
        @pl.when(p // n_cross != zl)
        def _():
            pl.semaphore_signal(barrier, inc=1, device_id=peer_z(p), device_id_type=MESH)
        return carry

    for p in range(n_mach):
        greet_m(p, 0)
    for p in range(n_cross):
        @pl.when(p != cross)
        def _():
            pl.semaphore_signal(barrier, inc=1, device_id=peer_c(p), device_id_type=MESH)
    for p in range(n_zl * n_cross):
        greet_b(p, 0)
    for q in range(n_core):
        @pl.when(q != core)
        def _():
            pl.semaphore_signal(barrier, inc=1, device_id=peer_core(q), device_id_type=MESH)

    nt = (((1,), (1,)), ((), ()))
    cross_f = cross_ref[...]
    mach_f = mach_ref[...]
    mach_w = mach_f.astype(jnp.float32)
    local_s[0] = lax.dot_general(mach_f, mach_f, nt, preferred_element_type=jnp.float32)
    local_s[2] = lax.dot_general(cross_f, cross_f, nt, preferred_element_type=jnp.float32)
    lane = lax.broadcasted_iota(jnp.int32, (rank, rolls_here), 1)
    terms_local = jnp.zeros((rank, rolls_here), jnp.float32)
    for k in range(n_chunks):
        loads[k].wait()
        for i in range(k * chunk, (k + 1) * chunk):
            value = lax.dot_general(cross_f, dens_v[i], nt, preferred_element_type=jnp.float32)
            part_ref[i] = value
            column = jnp.sum(value * mach_w, axis=1, keepdims=True)
            terms_local = jnp.where(lane == i, column, terms_local)
    local_s[1] = terms_local
    for k in range(3):
        for g in range(4):
            pay_ref[8 * k : 8 * k + 8, g * 32 : (g + 1) * 32] = local_s[k, pl.ds(g, 8, stride=4), :]

    pl.semaphore_wait(barrier, n_mach - 1 + n_cross - 1 + n_core - 1 + (n_zl - 1) * n_cross)

    def stage_1(p):
        return pltpu.make_async_remote_copy(
            src_ref=pay_ref.at[pl.ds(8, 16)], dst_ref=recv_1.at[cross], send_sem=send_1.at[p],
            recv_sem=got_1.at[cross], device_id=peer_c(p), device_id_type=MESH)

    def stage_1_in(p):
        return pltpu.make_async_remote_copy(
            src_ref=pay_ref.at[pl.ds(8, 16)], dst_ref=recv_1.at[p], send_sem=send_1.at[p],
            recv_sem=got_1.at[p], device_id=peer_c(p), device_id_type=MESH)

    for p in range(n_cross):
        @pl.when(p != cross)
        def _():
            stage_1(p).start()
    recv_1[cross] = pay_ref[8:24, :]
    for p in range(n_cross):
        @pl.when(p != cross)
        def _():
            stage_1_in(p).wait()
    terms = recv_1[0, 0:8, :]
    gc = recv_1[0, 8:16, :]
    for p in range(1, n_cross):
        terms = terms + recv_1[p, 0:8, :]
        gc = gc + recv_1[p, 8:16, :]

    pay_2[0:8, :] = pay_ref[0:8, :]
    pay_2[8:16, :] = terms

    def send_loop_2(p, carry):
        @pl.when(p != mach)
        def _():
            pltpu.make_async_remote_copy(
                src_ref=pay_2, dst_ref=recv_2.at[mach], send_sem=send_2.at[p], recv_sem=got_2.at[mach],
                device_id=peer_m(p), device_id_type=MESH).start()
        return carry

    def wait_loop_2(p, carry):
        @pl.when(p != mach)
        def _():
            pltpu.make_async_remote_copy(
                src_ref=pay_2, dst_ref=recv_2.at[p], send_sem=send_2.at[p], recv_sem=got_2.at[p],
                device_id=peer_m(p), device_id_type=MESH).wait()
        return carry

    for p in range(n_mach):
        send_loop_2(p, 0)
    recv_2[mach] = pay_2[...]
    for p in range(n_mach):
        wait_loop_2(p, 0)
    gm = recv_2[0, 0:8, :]
    terms = recv_2[0, 8:16, :]
    for p in range(1, n_mach):
        gm = gm + recv_2[p, 0:8, :]
        terms = terms + recv_2[p, 8:16, :]
    for g in range(4):
        lanes = slice(g * 32, (g + 1) * 32)
        gm_s[pl.ds(g, 8, stride=4), :] = gm[:, lanes]
        mt_s[pl.ds(g, 8, stride=4), :] = terms[:, lanes]
        gc_s[pl.ds(g, 8, stride=4), :] = gc[:, lanes]

    gram = gm_s[...] * gc_s[...]
    target = mt_s[...]
    rows = start_ref[...]
    mixed = gram[:, 0:1] * rows[0:1, :]
    for s_ in range(1, rank):
        mixed = mixed + gram[:, s_ : s_ + 1] * rows[s_ : s_ + 1, :]
    for r in range(rank):
        current = rows[r : r + 1, :]
        updated = jnp.maximum(current + (target[r : r + 1, :] - mixed[r : r + 1, :]) / gram[r : r + 1, r : r + 1], 0.0)
        rf_ref[r : r + 1, :] = updated
        mixed = mixed + gram[:, r : r + 1] * (updated - current)

    factor = rf_ref[...]
    bins_here_k = term_s.shape[0] * 128
    term = part_ref[0] * factor[:, 0:1]
    for i in range(1, part_ref.shape[0]):
        term = term + part_ref[i] * factor[:, i : i + 1]
    for t in range(term_s.shape[0]):
        term_s[t] = term[:, t * 128 : (t + 1) * 128]
    span = bins_here_k // n_cross
    per_row = 128 // span
    for c in range(n_cross):
        lo = (c * span) % 128
        for h in range(per_row):
            rows = term_s[(c * span) // 128, pl.ds(h, rank // per_row, stride=per_row), :]
            pieces[c, :, h * span : (h + 1) * span] = rows[:, lo : lo + span]

    for q in range(n_core):
        @pl.when(q != core)
        def _():
            pltpu.make_async_remote_copy(
                src_ref=pieces, dst_ref=recv_b1.at[core], send_sem=send_b1.at[q], recv_sem=got_b1.at[core],
                device_id=peer_core(q), device_id_type=MESH).start()
    recv_b1[core] = pieces[...]
    for q in range(n_core):
        @pl.when(q != core)
        def _():
            pltpu.make_async_remote_copy(
                src_ref=pieces, dst_ref=recv_b1.at[q], send_sem=send_b1.at[q], recv_sem=got_b1.at[q],
                device_id=peer_core(q), device_id_type=MESH).wait()
    summed = recv_b1[0]
    for q in range(1, n_core):
        summed = summed + recv_b1[q]
    core_sum[...] = summed

    for p in range(n_zl * n_cross):
        @pl.when(p != me_z)
        def _():
            pltpu.make_async_remote_copy(
                src_ref=core_sum.at[p % n_cross], dst_ref=recv_b2.at[me_z], send_sem=send_b2.at[p],
                recv_sem=got_b2.at[me_z], device_id=peer_z(p), device_id_type=MESH).start()
    recv_b2[me_z] = core_sum[cross]
    for p in range(n_zl * n_cross):
        @pl.when(p != me_z)
        def _():
            pltpu.make_async_remote_copy(
                src_ref=core_sum.at[p % n_cross], dst_ref=recv_b2.at[p], send_sem=send_b2.at[p],
                recv_sem=got_b2.at[p], device_id=peer_z(p), device_id_type=MESH).wait()

    total = recv_b2[0]
    for p in range(1, n_zl * n_cross):
        total = total + recv_b2[p]
    mode_ref[...] = total * scale


def finish_kernel(rf_ref, total_ref, rf_out, mode_out):
    rf_out[...] = rf_ref[...]
    span = mode_out.shape[1]
    per_row = 128 // span
    for r in range(mode_out.shape[0]):
        mode_out[r : r + 1, :] = total_ref[r // per_row : r // per_row + 1, (r % per_row) * span : (r % per_row + 1) * span]


def local(density, roll_start, mach_factor, cross_factor):
    rolls_here, bins_here, cross_here = density.shape
    rank = cross_factor.shape[0]
    n_roll = lax.axis_size("roll")
    n_mach = lax.axis_size("mach")
    n_cross = lax.axis_size("cross")
    n_chunks = 4
    n_core = 2 if n_roll % 2 == 0 else 1
    pay_rows = 3 * rank * rank // 128
    span = bins_here // n_cross
    scale = rank / (rolls_here * n_roll * cross_here * n_cross)
    roll_factor, mode_two = pl.pallas_call(
        functools.partial(fused_kernel, n_roll, n_cross, scale, n_chunks),
        out_shape=(
            jax.ShapeDtypeStruct(roll_start.shape, jnp.float32),
            jax.ShapeDtypeStruct((rank * span // 128, 128), jnp.float32),
        ),
        in_specs=[pl.BlockSpec(memory_space=pl.ANY)] + [pl.BlockSpec(memory_space=VMEM)] * 3,
        out_specs=[pl.BlockSpec(memory_space=VMEM)] * 2,
        scratch_shapes=[
            VMEM(density.shape, density.dtype),
            pltpu.SemaphoreType.DMA((n_chunks,)),
            VMEM((rolls_here, rank, bins_here), jnp.float32),
            VMEM((3, rank, rank), jnp.float32),
            VMEM((pay_rows, 128), jnp.float32),
            VMEM((n_cross, 16, 128), jnp.float32),
            pltpu.SemaphoreType.DMA((n_cross,)),
            pltpu.SemaphoreType.DMA((n_cross,)),
            VMEM((16, 128), jnp.float32),
            VMEM((n_mach, 16, 128), jnp.float32),
            pltpu.SemaphoreType.DMA((n_mach,)),
            pltpu.SemaphoreType.DMA((n_mach,)),
            VMEM((rank, rank), jnp.float32),
            VMEM((rank, rank), jnp.float32),
            VMEM((rank, rank), jnp.float32),
            VMEM((bins_here // 128, rank, 128), jnp.float32),
            VMEM((n_cross, rank * span // 128, 128), jnp.float32),
            VMEM((n_core, n_cross, rank * span // 128, 128), jnp.float32),
            pltpu.SemaphoreType.DMA((n_core,)),
            pltpu.SemaphoreType.DMA((n_core,)),
            VMEM((n_cross, rank * span // 128, 128), jnp.float32),
            VMEM((n_roll // n_core * n_cross, rank * span // 128, 128), jnp.float32),
            pltpu.SemaphoreType.DMA((n_roll // n_core * n_cross,)),
            pltpu.SemaphoreType.DMA((n_roll // n_core * n_cross,)),
        ],
        compiler_params=pltpu.CompilerParams(collective_id=0, has_side_effects=True),
    )(density, cross_factor, mach_factor, roll_start)
    return pl.pallas_call(
        finish_kernel,
        out_shape=(
            jax.ShapeDtypeStruct(roll_start.shape, jnp.float32),
            jax.ShapeDtypeStruct((rank, span), jnp.float32),
        ),
        in_specs=[pl.BlockSpec(memory_space=VMEM)] * 2,
        out_specs=[pl.BlockSpec(memory_space=VMEM)] * 2,
    )(roll_factor, mode_two)


def solution(mesh):
    in_specs = (P("roll", "mach", "cross"), P(None, "roll"), P(None, "mach"), P(None, "cross"))
    out_specs = (P(None, "roll"), P(None, ("mach", "cross")))
    return jax.shard_map(local, mesh=mesh, in_specs=in_specs, out_specs=out_specs, check_vma=False)
```

```python
import functools

import jax
import jax.numpy as jnp
from jax import lax
from jax.experimental import pallas as pl
from jax.experimental.pallas import tpu as pltpu
from jax.sharding import PartitionSpec as P

MESH = pl.DeviceIdType.MESH
VMEM = pltpu.VMEM


def fused_kernel(n_roll, n_cross, scale, n_chunks, dens_hbm, cross_ref, mach_ref, start_ref, rf_ref, mode_ref,
                 dens_v, dens_sem, part_ref, local_s, pay_ref,
                 recv_1, send_1, got_1, pay_2, recv_2, send_2, got_2, gm_s, mt_s, gc_s, term_s, pieces, recv_b, send_b, got_b):
    roll = lax.axis_index("roll")
    mach = lax.axis_index("mach")
    cross = lax.axis_index("cross")
    n_mach = recv_2.shape[0]
    group_b = recv_b.shape[0]
    me_b = roll * n_cross + cross
    rank = rf_ref.shape[0]

    def peer_c(p):
        return (roll, mach, p)

    def peer_m(p):
        return (roll, p, cross)

    def peer_b(p):
        return (p // n_cross, mach, p % n_cross)

    rolls_here = dens_v.shape[0]
    chunk = rolls_here // n_chunks
    loads = [
        pltpu.make_async_copy(dens_hbm.at[pl.ds(k * chunk, chunk)], dens_v.at[pl.ds(k * chunk, chunk)], dens_sem.at[k])
        for k in range(n_chunks)
    ]
    for load in loads:
        load.start()

    barrier = pltpu.get_barrier_semaphore()

    def greet_m(p, carry):
        @pl.when(p != mach)
        def _():
            pl.semaphore_signal(barrier, inc=1, device_id=peer_m(p), device_id_type=MESH)
        return carry

    def greet_b(p, carry):
        @pl.when(p // n_cross != roll)
        def _():
            pl.semaphore_signal(barrier, inc=1, device_id=peer_b(p), device_id_type=MESH)
        return carry

    for p in range(n_mach):
        greet_m(p, 0)
    for p in range(n_cross):
        @pl.when(p != cross)
        def _():
            pl.semaphore_signal(barrier, inc=1, device_id=peer_c(p), device_id_type=MESH)
    for p in range(group_b):
        greet_b(p, 0)

    nt = (((1,), (1,)), ((), ()))
    cross_f = cross_ref[...]
    mach_f = mach_ref[...]
    mach_w = mach_f.astype(jnp.float32)
    local_s[0] = lax.dot_general(mach_f, mach_f, nt, preferred_element_type=jnp.float32)
    local_s[2] = lax.dot_general(cross_f, cross_f, nt, preferred_element_type=jnp.float32)
    lane = lax.broadcasted_iota(jnp.int32, (rank, rolls_here), 1)
    terms_local = jnp.zeros((rank, rolls_here), jnp.float32)
    for k in range(n_chunks):
        loads[k].wait()
        for i in range(k * chunk, (k + 1) * chunk):
            value = lax.dot_general(cross_f, dens_v[i], nt, preferred_element_type=jnp.float32)
            part_ref[i] = value
            column = jnp.sum(value * mach_w, axis=1, keepdims=True)
            terms_local = jnp.where(lane == i, column, terms_local)
    local_s[1] = terms_local
    for k in range(3):
        for g in range(4):
            pay_ref[8 * k : 8 * k + 8, g * 32 : (g + 1) * 32] = local_s[k, pl.ds(g, 8, stride=4), :]

    pl.semaphore_wait(barrier, n_mach - 1 + group_b - 1)

    def stage_1(p):
        return pltpu.make_async_remote_copy(
            src_ref=pay_ref.at[pl.ds(8, 16)], dst_ref=recv_1.at[cross], send_sem=send_1.at[p],
            recv_sem=got_1.at[cross], device_id=peer_c(p), device_id_type=MESH)

    def stage_1_in(p):
        return pltpu.make_async_remote_copy(
            src_ref=pay_ref.at[pl.ds(8, 16)], dst_ref=recv_1.at[p], send_sem=send_1.at[p],
            recv_sem=got_1.at[p], device_id=peer_c(p), device_id_type=MESH)

    for p in range(n_cross):
        @pl.when(p != cross)
        def _():
            stage_1(p).start()
    recv_1[cross] = pay_ref[8:24, :]
    for p in range(n_cross):
        @pl.when(p != cross)
        def _():
            stage_1_in(p).wait()
    terms = recv_1[0, 0:8, :]
    gc = recv_1[0, 8:16, :]
    for p in range(1, n_cross):
        terms = terms + recv_1[p, 0:8, :]
        gc = gc + recv_1[p, 8:16, :]

    pay_2[0:8, :] = pay_ref[0:8, :]
    pay_2[8:16, :] = terms

    def send_loop_2(p, carry):
        @pl.when(p != mach)
        def _():
            pltpu.make_async_remote_copy(
                src_ref=pay_2, dst_ref=recv_2.at[mach], send_sem=send_2.at[p], recv_sem=got_2.at[mach],
                device_id=peer_m(p), device_id_type=MESH).start()
        return carry

    def wait_loop_2(p, carry):
        @pl.when(p != mach)
        def _():
            pltpu.make_async_remote_copy(
                src_ref=pay_2, dst_ref=recv_2.at[p], send_sem=send_2.at[p], recv_sem=got_2.at[p],
                device_id=peer_m(p), device_id_type=MESH).wait()
        return carry

    for p in range(n_mach):
        send_loop_2(p, 0)
    recv_2[mach] = pay_2[...]
    for p in range(n_mach):
        wait_loop_2(p, 0)
    gm = recv_2[0, 0:8, :]
    terms = recv_2[0, 8:16, :]
    for p in range(1, n_mach):
        gm = gm + recv_2[p, 0:8, :]
        terms = terms + recv_2[p, 8:16, :]
    for g in range(4):
        lanes = slice(g * 32, (g + 1) * 32)
        gm_s[pl.ds(g, 8, stride=4), :] = gm[:, lanes]
        mt_s[pl.ds(g, 8, stride=4), :] = terms[:, lanes]
        gc_s[pl.ds(g, 8, stride=4), :] = gc[:, lanes]

    gram = gm_s[...] * gc_s[...]
    target = mt_s[...]
    rows = start_ref[...]
    mixed = gram[:, 0:1] * rows[0:1, :]
    for s_ in range(1, rank):
        mixed = mixed + gram[:, s_ : s_ + 1] * rows[s_ : s_ + 1, :]
    bins_here_k = term_s.shape[0] * 128

    def term_block(lo):
        factor = rf_ref[lo : lo + 8, :]
        term = part_ref[0, lo : lo + 8, :] * factor[:, 0:1]
        for i in range(1, part_ref.shape[0]):
            term = term + part_ref[i, lo : lo + 8, :] * factor[:, i : i + 1]
        for t in range(term_s.shape[0]):
            term_s[t, lo : lo + 8, :] = term[:, t * 128 : (t + 1) * 128]

    for r in range(rank):
        current = rows[r : r + 1, :]
        updated = jnp.maximum(current + (target[r : r + 1, :] - mixed[r : r + 1, :]) / gram[r : r + 1, r : r + 1], 0.0)
        rf_ref[r : r + 1, :] = updated
        mixed = mixed + gram[:, r : r + 1] * (updated - current)
        if r % 8 == 7:
            term_block(r - 7)

    span = bins_here_k // n_cross
    per_row = 128 // span
    for c in range(n_cross):
        lo = (c * span) % 128
        for h in range(per_row):
            rows = term_s[(c * span) // 128, pl.ds(h, rank // per_row, stride=per_row), :]
            pieces[c, :, h * span : (h + 1) * span] = rows[:, lo : lo + span]

    def send_loop_b(p, carry):
        @pl.when(p != me_b)
        def _():
            pltpu.make_async_remote_copy(
                src_ref=pieces.at[p % n_cross], dst_ref=recv_b.at[me_b],
                send_sem=send_b.at[p], recv_sem=got_b.at[me_b], device_id=peer_b(p), device_id_type=MESH,
            ).start()
        return carry

    def wait_loop_b(p, carry):
        @pl.when(p != me_b)
        def _():
            pltpu.make_async_remote_copy(
                src_ref=pieces.at[p % n_cross], dst_ref=recv_b.at[p],
                send_sem=send_b.at[p], recv_sem=got_b.at[p], device_id=peer_b(p), device_id_type=MESH,
            ).wait()
        return carry

    for p in range(group_b):
        send_loop_b(p, 0)
    recv_b[me_b] = pieces[cross]
    for p in range(group_b):
        wait_loop_b(p, 0)

    total = recv_b[0]
    for p in range(1, group_b):
        total = total + recv_b[p]
    mode_ref[...] = total * scale


def finish_kernel(rf_ref, total_ref, rf_out, mode_out):
    rf_out[...] = rf_ref[...]
    span = mode_out.shape[1]
    per_row = 128 // span
    for r in range(mode_out.shape[0]):
        mode_out[r : r + 1, :] = total_ref[r // per_row : r // per_row + 1, (r % per_row) * span : (r % per_row + 1) * span]


def local(density, roll_start, mach_factor, cross_factor):
    rolls_here, bins_here, cross_here = density.shape
    rank = cross_factor.shape[0]
    n_roll = lax.axis_size("roll")
    n_mach = lax.axis_size("mach")
    n_cross = lax.axis_size("cross")
    n_chunks = 4
    pay_rows = 3 * rank * rank // 128
    span = bins_here // n_cross
    scale = rank / (rolls_here * n_roll * cross_here * n_cross)
    roll_factor, mode_two = pl.pallas_call(
        functools.partial(fused_kernel, n_roll, n_cross, scale, n_chunks),
        out_shape=(
            jax.ShapeDtypeStruct(roll_start.shape, jnp.float32),
            jax.ShapeDtypeStruct((rank * span // 128, 128), jnp.float32),
        ),
        in_specs=[pl.BlockSpec(memory_space=pl.ANY)] + [pl.BlockSpec(memory_space=VMEM)] * 3,
        out_specs=[pl.BlockSpec(memory_space=VMEM)] * 2,
        scratch_shapes=[
            VMEM(density.shape, density.dtype),
            pltpu.SemaphoreType.DMA((n_chunks,)),
            VMEM((rolls_here, rank, bins_here), jnp.float32),
            VMEM((3, rank, rank), jnp.float32),
            VMEM((pay_rows, 128), jnp.float32),
            VMEM((n_cross, 16, 128), jnp.float32),
            pltpu.SemaphoreType.DMA((n_cross,)),
            pltpu.SemaphoreType.DMA((n_cross,)),
            VMEM((16, 128), jnp.float32),
            VMEM((n_mach, 16, 128), jnp.float32),
            pltpu.SemaphoreType.DMA((n_mach,)),
            pltpu.SemaphoreType.DMA((n_mach,)),
            VMEM((rank, rank), jnp.float32),
            VMEM((rank, rank), jnp.float32),
            VMEM((rank, rank), jnp.float32),
            VMEM((bins_here // 128, rank, 128), jnp.float32),
            VMEM((n_cross, rank * span // 128, 128), jnp.float32),
            VMEM((n_roll * n_cross, rank * span // 128, 128), jnp.float32),
            pltpu.SemaphoreType.DMA((n_roll * n_cross,)),
            pltpu.SemaphoreType.DMA((n_roll * n_cross,)),
        ],
        compiler_params=pltpu.CompilerParams(collective_id=0, has_side_effects=True),
    )(density, cross_factor, mach_factor, roll_start)
    return pl.pallas_call(
        finish_kernel,
        out_shape=(
            jax.ShapeDtypeStruct(roll_start.shape, jnp.float32),
            jax.ShapeDtypeStruct((rank, span), jnp.float32),
        ),
        in_specs=[pl.BlockSpec(memory_space=VMEM)] * 2,
        out_specs=[pl.BlockSpec(memory_space=VMEM)] * 2,
    )(roll_factor, mode_two)


def solution(mesh):
    in_specs = (P("roll", "mach", "cross"), P(None, "roll"), P(None, "mach"), P(None, "cross"))
    out_specs = (P(None, "roll"), P(None, ("mach", "cross")))
    return jax.shard_map(local, mesh=mesh, in_specs=in_specs, out_specs=out_specs, check_vma=False)
```

```python
import functools

import jax
import jax.numpy as jnp
from jax import lax
from jax.experimental import pallas as pl
from jax.experimental.pallas import tpu as pltpu
from jax.sharding import PartitionSpec as P

MESH = pl.DeviceIdType.MESH
VMEM = pltpu.VMEM


def fused_kernel(n_roll, n_cross, scale, n_chunks, dens_hbm, cross_ref, mach_ref, start_ref, rf_ref, mode_ref,
                 dens_v, dens_sem, part_ref, local_s, pay_ref,
                 recv_1, send_1, got_1, pay_2, recv_2, send_2, got_2, gm_s, mt_s, gc_s, term_s, pieces, recv_b, send_b, got_b):
    roll = lax.axis_index("roll")
    mach = lax.axis_index("mach")
    cross = lax.axis_index("cross")
    n_mach = recv_2.shape[0]
    group_b = recv_b.shape[0]
    me_b = roll * n_cross + cross
    rank = rf_ref.shape[0]

    def peer_c(p):
        return (roll, mach, p)

    def peer_m(p):
        return (roll, p, cross)

    def peer_b(p):
        return (p // n_cross, mach, p % n_cross)

    rolls_here = dens_v.shape[0]
    chunk = rolls_here // n_chunks
    loads = [
        pltpu.make_async_copy(dens_hbm.at[pl.ds(k * chunk, chunk)], dens_v.at[pl.ds(k * chunk, chunk)], dens_sem.at[k])
        for k in range(n_chunks)
    ]
    for load in loads:
        load.start()

    barrier = pltpu.get_barrier_semaphore()

    def greet_m(p, carry):
        @pl.when(p != mach)
        def _():
            pl.semaphore_signal(barrier, inc=1, device_id=peer_m(p), device_id_type=MESH)
        return carry

    def greet_b(p, carry):
        @pl.when(p // n_cross != roll)
        def _():
            pl.semaphore_signal(barrier, inc=1, device_id=peer_b(p), device_id_type=MESH)
        return carry

    for p in range(n_mach):
        greet_m(p, 0)
    for p in range(n_cross):
        @pl.when(p != cross)
        def _():
            pl.semaphore_signal(barrier, inc=1, device_id=peer_c(p), device_id_type=MESH)
    for p in range(group_b):
        greet_b(p, 0)

    nt = (((1,), (1,)), ((), ()))
    cross_f = cross_ref[...]
    mach_f = mach_ref[...]
    mach_w = mach_f.astype(jnp.float32)
    local_s[0] = lax.dot_general(mach_f, mach_f, nt, preferred_element_type=jnp.float32)
    local_s[2] = lax.dot_general(cross_f, cross_f, nt, preferred_element_type=jnp.float32)
    lane = lax.broadcasted_iota(jnp.int32, (rank, rolls_here), 1)
    terms_local = jnp.zeros((rank, rolls_here), jnp.float32)
    for k in range(n_chunks):
        loads[k].wait()
        for i in range(k * chunk, (k + 1) * chunk):
            value = lax.dot_general(cross_f, dens_v[i], nt, preferred_element_type=jnp.float32)
            part_ref[i] = value
            column = jnp.sum(value * mach_w, axis=1, keepdims=True)
            terms_local = jnp.where(lane == i, column, terms_local)
    local_s[1] = terms_local
    for k in range(3):
        for g in range(4):
            pay_ref[8 * k : 8 * k + 8, g * 32 : (g + 1) * 32] = local_s[k, pl.ds(g, 8, stride=4), :]

    pl.semaphore_wait(barrier, n_mach - 1 + group_b - 1)

    def stage_1(p):
        return pltpu.make_async_remote_copy(
            src_ref=pay_ref.at[pl.ds(8, 16)], dst_ref=recv_1.at[cross], send_sem=send_1.at[p],
            recv_sem=got_1.at[cross], device_id=peer_c(p), device_id_type=MESH)

    def stage_1_in(p):
        return pltpu.make_async_remote_copy(
            src_ref=pay_ref.at[pl.ds(8, 16)], dst_ref=recv_1.at[p], send_sem=send_1.at[p],
            recv_sem=got_1.at[p], device_id=peer_c(p), device_id_type=MESH)

    for p in range(n_cross):
        @pl.when(p != cross)
        def _():
            stage_1(p).start()
    recv_1[cross] = pay_ref[8:24, :]
    for p in range(n_cross):
        @pl.when(p != cross)
        def _():
            stage_1_in(p).wait()
    terms = recv_1[0, 0:8, :]
    gc = recv_1[0, 8:16, :]
    for p in range(1, n_cross):
        terms = terms + recv_1[p, 0:8, :]
        gc = gc + recv_1[p, 8:16, :]

    pay_2[0:8, :] = pay_ref[0:8, :]
    pay_2[8:16, :] = terms

    def send_loop_2(p, carry):
        @pl.when(p != mach)
        def _():
            pltpu.make_async_remote_copy(
                src_ref=pay_2, dst_ref=recv_2.at[mach], send_sem=send_2.at[p], recv_sem=got_2.at[mach],
                device_id=peer_m(p), device_id_type=MESH).start()
        return carry

    def wait_loop_2(p, carry):
        @pl.when(p != mach)
        def _():
            pltpu.make_async_remote_copy(
                src_ref=pay_2, dst_ref=recv_2.at[p], send_sem=send_2.at[p], recv_sem=got_2.at[p],
                device_id=peer_m(p), device_id_type=MESH).wait()
        return carry

    for p in range(n_mach):
        send_loop_2(p, 0)
    recv_2[mach] = pay_2[...]
    for p in range(n_mach):
        wait_loop_2(p, 0)
    gm = recv_2[0, 0:8, :]
    terms = recv_2[0, 8:16, :]
    for p in range(1, n_mach):
        gm = gm + recv_2[p, 0:8, :]
        terms = terms + recv_2[p, 8:16, :]
    for g in range(4):
        lanes = slice(g * 32, (g + 1) * 32)
        gm_s[pl.ds(g, 8, stride=4), :] = gm[:, lanes]
        mt_s[pl.ds(g, 8, stride=4), :] = terms[:, lanes]
        gc_s[pl.ds(g, 8, stride=4), :] = gc[:, lanes]

    gram = gm_s[...] * gc_s[...]
    target = mt_s[...]
    rows = start_ref[...]
    mixed = gram[:, 0:1] * rows[0:1, :]
    for s_ in range(1, rank):
        mixed = mixed + gram[:, s_ : s_ + 1] * rows[s_ : s_ + 1, :]
    for r in range(rank):
        current = rows[r : r + 1, :]
        updated = jnp.maximum(current + (target[r : r + 1, :] - mixed[r : r + 1, :]) / gram[r : r + 1, r : r + 1], 0.0)
        rf_ref[r : r + 1, :] = updated
        mixed = mixed + gram[:, r : r + 1] * (updated - current)

    factor = rf_ref[...]
    bins_here_k = term_s.shape[0] * 128
    term = part_ref[0] * factor[:, 0:1]
    for i in range(1, part_ref.shape[0]):
        term = term + part_ref[i] * factor[:, i : i + 1]
    for t in range(term_s.shape[0]):
        term_s[t] = term[:, t * 128 : (t + 1) * 128]
    span = bins_here_k // n_cross
    per_row = 128 // span
    for c in range(n_cross):
        lo = (c * span) % 128
        for h in range(per_row):
            rows = term_s[(c * span) // 128, pl.ds(h, rank // per_row, stride=per_row), :]
            pieces[c, :, h * span : (h + 1) * span] = rows[:, lo : lo + span]

    def send_loop_b(p, carry):
        @pl.when(p != me_b)
        def _():
            pltpu.make_async_remote_copy(
                src_ref=pieces.at[p % n_cross], dst_ref=recv_b.at[me_b],
                send_sem=send_b.at[p], recv_sem=got_b.at[me_b], device_id=peer_b(p), device_id_type=MESH,
            ).start()
        return carry

    def wait_loop_b(p, carry):
        @pl.when(p != me_b)
        def _():
            pltpu.make_async_remote_copy(
                src_ref=pieces.at[p % n_cross], dst_ref=recv_b.at[p],
                send_sem=send_b.at[p], recv_sem=got_b.at[p], device_id=peer_b(p), device_id_type=MESH,
            ).wait()
        return carry

    for p in range(group_b):
        send_loop_b(p, 0)
    recv_b[me_b] = pieces[cross]
    for p in range(group_b):
        wait_loop_b(p, 0)

    total = recv_b[0]
    for p in range(1, group_b):
        total = total + recv_b[p]
    total = total * scale
    span = mode_ref.shape[1]
    per_row = 128 // span
    for h in range(per_row):
        mode_ref[pl.ds(h, rank // per_row, stride=per_row), :] = total[:, h * span : (h + 1) * span]


def finish_kernel(rf_ref, mode_ref, rf_out, mode_out, sems):
    copies = [
        pltpu.make_async_copy(rf_ref, rf_out, sems.at[0]),
        pltpu.make_async_copy(mode_ref, mode_out, sems.at[1]),
    ]
    for copy in copies:
        copy.start()
    for copy in copies:
        copy.wait()


def local(density, roll_start, mach_factor, cross_factor):
    rolls_here, bins_here, cross_here = density.shape
    rank = cross_factor.shape[0]
    n_roll = lax.axis_size("roll")
    n_mach = lax.axis_size("mach")
    n_cross = lax.axis_size("cross")
    n_chunks = 4
    pay_rows = 3 * rank * rank // 128
    span = bins_here // n_cross
    scale = rank / (rolls_here * n_roll * cross_here * n_cross)
    roll_factor, mode_two = pl.pallas_call(
        functools.partial(fused_kernel, n_roll, n_cross, scale, n_chunks),
        out_shape=(
            jax.ShapeDtypeStruct(roll_start.shape, jnp.float32),
            jax.ShapeDtypeStruct((rank, span), jnp.float32),
        ),
        in_specs=[pl.BlockSpec(memory_space=pl.ANY)] + [pl.BlockSpec(memory_space=VMEM)] * 3,
        out_specs=[pl.BlockSpec(memory_space=VMEM)] * 2,
        scratch_shapes=[
            VMEM(density.shape, density.dtype),
            pltpu.SemaphoreType.DMA((n_chunks,)),
            VMEM((rolls_here, rank, bins_here), jnp.float32),
            VMEM((3, rank, rank), jnp.float32),
            VMEM((pay_rows, 128), jnp.float32),
            VMEM((n_cross, 16, 128), jnp.float32),
            pltpu.SemaphoreType.DMA((n_cross,)),
            pltpu.SemaphoreType.DMA((n_cross,)),
            VMEM((16, 128), jnp.float32),
            VMEM((n_mach, 16, 128), jnp.float32),
            pltpu.SemaphoreType.DMA((n_mach,)),
            pltpu.SemaphoreType.DMA((n_mach,)),
            VMEM((rank, rank), jnp.float32),
            VMEM((rank, rank), jnp.float32),
            VMEM((rank, rank), jnp.float32),
            VMEM((bins_here // 128, rank, 128), jnp.float32),
            VMEM((n_cross, rank * span // 128, 128), jnp.float32),
            VMEM((n_roll * n_cross, rank * span // 128, 128), jnp.float32),
            pltpu.SemaphoreType.DMA((n_roll * n_cross,)),
            pltpu.SemaphoreType.DMA((n_roll * n_cross,)),
        ],
        compiler_params=pltpu.CompilerParams(collective_id=0, has_side_effects=True),
    )(density, cross_factor, mach_factor, roll_start)
    return pl.pallas_call(
        finish_kernel,
        out_shape=(
            jax.ShapeDtypeStruct(roll_start.shape, jnp.float32),
            jax.ShapeDtypeStruct((rank, span), jnp.float32),
        ),
        in_specs=[pl.BlockSpec(memory_space=pl.ANY)] * 2,
        out_specs=[pl.BlockSpec(memory_space=pl.ANY)] * 2,
        scratch_shapes=[pltpu.SemaphoreType.DMA((2,))],
    )(roll_factor, mode_two)


def solution(mesh):
    in_specs = (P("roll", "mach", "cross"), P(None, "roll"), P(None, "mach"), P(None, "cross"))
    out_specs = (P(None, "roll"), P(None, ("mach", "cross")))
    return jax.shard_map(local, mesh=mesh, in_specs=in_specs, out_specs=out_specs, check_vma=False)
```

```python
import functools

import jax
import jax.numpy as jnp
from jax import lax
from jax.experimental import pallas as pl
from jax.experimental.pallas import tpu as pltpu
from jax.sharding import PartitionSpec as P

MESH = pl.DeviceIdType.MESH
VMEM = pltpu.VMEM


def fused_kernel(n_roll, n_cross, scale, n_chunks, dens_hbm, cross_ref, mach_ref, start_ref, rf_ref, mode_ref,
                 dens_v, dens_sem, part_ref, local_s, pay_ref,
                 recv_1, send_1, got_1, pay_2, recv_2, send_2, got_2, gm_s, mt_s, gc_s, term_s, pieces, recv_b, send_b, got_b):
    roll = lax.axis_index("roll")
    mach = lax.axis_index("mach")
    cross = lax.axis_index("cross")
    n_mach = recv_2.shape[0]
    group_b = recv_b.shape[0]
    me_b = roll * n_cross + cross
    rank = rf_ref.shape[0]

    def peer_c(p):
        return (roll, mach, p)

    def peer_m(p):
        return (roll, p, cross)

    def peer_b(p):
        return (p // n_cross, mach, p % n_cross)

    rolls_here = dens_v.shape[0]
    chunk = rolls_here // n_chunks
    loads = [
        pltpu.make_async_copy(dens_hbm.at[pl.ds(k * chunk, chunk)], dens_v.at[pl.ds(k * chunk, chunk)], dens_sem.at[k])
        for k in range(n_chunks)
    ]
    for load in loads:
        load.start()

    barrier = pltpu.get_barrier_semaphore()

    def greet_m(p, carry):
        @pl.when(p != mach)
        def _():
            pl.semaphore_signal(barrier, inc=1, device_id=peer_m(p), device_id_type=MESH)
        return carry

    def greet_b(p, carry):
        @pl.when(p // n_cross != roll)
        def _():
            pl.semaphore_signal(barrier, inc=1, device_id=peer_b(p), device_id_type=MESH)
        return carry

    for p in range(n_mach):
        greet_m(p, 0)
    for p in range(n_cross):
        @pl.when(p != cross)
        def _():
            pl.semaphore_signal(barrier, inc=1, device_id=peer_c(p), device_id_type=MESH)
    for p in range(group_b):
        greet_b(p, 0)

    nt = (((1,), (1,)), ((), ()))
    cross_f = cross_ref[...]
    mach_f = mach_ref[...]
    mach_w = mach_f.astype(jnp.float32)
    local_s[0] = lax.dot_general(mach_f, mach_f, nt, preferred_element_type=jnp.float32)
    local_s[2] = lax.dot_general(cross_f, cross_f, nt, preferred_element_type=jnp.float32)
    lane = lax.broadcasted_iota(jnp.int32, (rank, rolls_here), 1)
    terms_local = jnp.zeros((rank, rolls_here), jnp.float32)
    for k in range(n_chunks):
        loads[k].wait()
        for i in range(k * chunk, (k + 1) * chunk):
            value = lax.dot_general(cross_f, dens_v[i], nt, preferred_element_type=jnp.float32)
            part_ref[i] = value
            column = jnp.sum(value * mach_w, axis=1, keepdims=True)
            terms_local = jnp.where(lane == i, column, terms_local)
    local_s[1] = terms_local
    for k in range(3):
        for g in range(4):
            pay_ref[8 * k : 8 * k + 8, g * 32 : (g + 1) * 32] = local_s[k, pl.ds(g, 8, stride=4), :]

    pl.semaphore_wait(barrier, n_mach - 1 + group_b - 1)

    def stage_1(p):
        return pltpu.make_async_remote_copy(
            src_ref=pay_ref.at[pl.ds(8, 16)], dst_ref=recv_1.at[cross], send_sem=send_1.at[p],
            recv_sem=got_1.at[cross], device_id=peer_c(p), device_id_type=MESH)

    def stage_1_in(p):
        return pltpu.make_async_remote_copy(
            src_ref=pay_ref.at[pl.ds(8, 16)], dst_ref=recv_1.at[p], send_sem=send_1.at[p],
            recv_sem=got_1.at[p], device_id=peer_c(p), device_id_type=MESH)

    for p in range(n_cross):
        @pl.when(p != cross)
        def _():
            stage_1(p).start()
    for p in range(n_mach):
        @pl.when(p != mach)
        def _():
            pltpu.make_async_remote_copy(
                src_ref=pay_ref.at[pl.ds(0, 8)], dst_ref=recv_2.at[mach, pl.ds(0, 8)], send_sem=send_2.at[p],
                recv_sem=got_2.at[mach], device_id=peer_m(p), device_id_type=MESH).start()
    recv_1[cross] = pay_ref[8:24, :]
    for p in range(n_cross):
        @pl.when(p != cross)
        def _():
            stage_1_in(p).wait()
    terms = recv_1[0, 0:8, :]
    gc = recv_1[0, 8:16, :]
    for p in range(1, n_cross):
        terms = terms + recv_1[p, 0:8, :]
        gc = gc + recv_1[p, 8:16, :]

    pay_2[8:16, :] = terms

    def send_loop_2(p, carry):
        @pl.when(p != mach)
        def _():
            pltpu.make_async_remote_copy(
                src_ref=pay_2.at[pl.ds(8, 8)], dst_ref=recv_2.at[mach, pl.ds(8, 8)], send_sem=send_2.at[p],
                recv_sem=got_2.at[mach], device_id=peer_m(p), device_id_type=MESH).start()
        return carry

    def wait_loop_2(p, carry):
        @pl.when(p != mach)
        def _():
            pltpu.make_async_remote_copy(
                src_ref=pay_2, dst_ref=recv_2.at[p], send_sem=send_2.at[p], recv_sem=got_2.at[p],
                device_id=peer_m(p), device_id_type=MESH).wait()
        return carry

    for p in range(n_mach):
        send_loop_2(p, 0)
    recv_2[mach, 0:8, :] = pay_ref[0:8, :]
    recv_2[mach, 8:16, :] = terms
    for p in range(n_mach):
        wait_loop_2(p, 0)
    gm = recv_2[0, 0:8, :]
    terms = recv_2[0, 8:16, :]
    for p in range(1, n_mach):
        gm = gm + recv_2[p, 0:8, :]
        terms = terms + recv_2[p, 8:16, :]
    for g in range(4):
        lanes = slice(g * 32, (g + 1) * 32)
        gm_s[pl.ds(g, 8, stride=4), :] = gm[:, lanes]
        mt_s[pl.ds(g, 8, stride=4), :] = terms[:, lanes]
        gc_s[pl.ds(g, 8, stride=4), :] = gc[:, lanes]

    gram = gm_s[...] * gc_s[...]
    target = mt_s[...]
    rows = start_ref[...]
    mixed = gram[:, 0:1] * rows[0:1, :]
    for s_ in range(1, rank):
        mixed = mixed + gram[:, s_ : s_ + 1] * rows[s_ : s_ + 1, :]
    for r in range(rank):
        current = rows[r : r + 1, :]
        updated = jnp.maximum(current + (target[r : r + 1, :] - mixed[r : r + 1, :]) / gram[r : r + 1, r : r + 1], 0.0)
        rf_ref[r : r + 1, :] = updated
        mixed = mixed + gram[:, r : r + 1] * (updated - current)

    factor = rf_ref[...]
    bins_here_k = term_s.shape[0] * 128
    term = part_ref[0] * factor[:, 0:1]
    for i in range(1, part_ref.shape[0]):
        term = term + part_ref[i] * factor[:, i : i + 1]
    for t in range(term_s.shape[0]):
        term_s[t] = term[:, t * 128 : (t + 1) * 128]
    span = bins_here_k // n_cross
    per_row = 128 // span
    for c in range(n_cross):
        lo = (c * span) % 128
        for h in range(per_row):
            rows = term_s[(c * span) // 128, pl.ds(h, rank // per_row, stride=per_row), :]
            pieces[c, :, h * span : (h + 1) * span] = rows[:, lo : lo + span]

    def send_loop_b(p, carry):
        @pl.when(p != me_b)
        def _():
            pltpu.make_async_remote_copy(
                src_ref=pieces.at[p % n_cross], dst_ref=recv_b.at[me_b],
                send_sem=send_b.at[p], recv_sem=got_b.at[me_b], device_id=peer_b(p), device_id_type=MESH,
            ).start()
        return carry

    def wait_loop_b(p, carry):
        @pl.when(p != me_b)
        def _():
            pltpu.make_async_remote_copy(
                src_ref=pieces.at[p % n_cross], dst_ref=recv_b.at[p],
                send_sem=send_b.at[p], recv_sem=got_b.at[p], device_id=peer_b(p), device_id_type=MESH,
            ).wait()
        return carry

    for p in range(group_b):
        send_loop_b(p, 0)
    recv_b[me_b] = pieces[cross]
    for p in range(group_b):
        wait_loop_b(p, 0)

    total = recv_b[0]
    for p in range(1, group_b):
        total = total + recv_b[p]
    mode_ref[...] = total * scale


def finish_kernel(rf_ref, total_ref, rf_out, mode_out):
    rf_out[...] = rf_ref[...]
    span = mode_out.shape[1]
    per_row = 128 // span
    for r in range(mode_out.shape[0]):
        mode_out[r : r + 1, :] = total_ref[r // per_row : r // per_row + 1, (r % per_row) * span : (r % per_row + 1) * span]


def local(density, roll_start, mach_factor, cross_factor):
    rolls_here, bins_here, cross_here = density.shape
    rank = cross_factor.shape[0]
    n_roll = lax.axis_size("roll")
    n_mach = lax.axis_size("mach")
    n_cross = lax.axis_size("cross")
    n_chunks = 4
    pay_rows = 3 * rank * rank // 128
    span = bins_here // n_cross
    scale = rank / (rolls_here * n_roll * cross_here * n_cross)
    roll_factor, mode_two = pl.pallas_call(
        functools.partial(fused_kernel, n_roll, n_cross, scale, n_chunks),
        out_shape=(
            jax.ShapeDtypeStruct(roll_start.shape, jnp.float32),
            jax.ShapeDtypeStruct((rank * span // 128, 128), jnp.float32),
        ),
        in_specs=[pl.BlockSpec(memory_space=pl.ANY)] + [pl.BlockSpec(memory_space=VMEM)] * 3,
        out_specs=[pl.BlockSpec(memory_space=VMEM)] * 2,
        scratch_shapes=[
            VMEM(density.shape, density.dtype),
            pltpu.SemaphoreType.DMA((n_chunks,)),
            VMEM((rolls_here, rank, bins_here), jnp.float32),
            VMEM((3, rank, rank), jnp.float32),
            VMEM((pay_rows, 128), jnp.float32),
            VMEM((n_cross, 16, 128), jnp.float32),
            pltpu.SemaphoreType.DMA((n_cross,)),
            pltpu.SemaphoreType.DMA((n_cross,)),
            VMEM((16, 128), jnp.float32),
            VMEM((n_mach, 16, 128), jnp.float32),
            pltpu.SemaphoreType.DMA((n_mach,)),
            pltpu.SemaphoreType.DMA((n_mach,)),
            VMEM((rank, rank), jnp.float32),
            VMEM((rank, rank), jnp.float32),
            VMEM((rank, rank), jnp.float32),
            VMEM((bins_here // 128, rank, 128), jnp.float32),
            VMEM((n_cross, rank * span // 128, 128), jnp.float32),
            VMEM((n_roll * n_cross, rank * span // 128, 128), jnp.float32),
            pltpu.SemaphoreType.DMA((n_roll * n_cross,)),
            pltpu.SemaphoreType.DMA((n_roll * n_cross,)),
        ],
        compiler_params=pltpu.CompilerParams(collective_id=0, has_side_effects=True),
    )(density, cross_factor, mach_factor, roll_start)
    return pl.pallas_call(
        finish_kernel,
        out_shape=(
            jax.ShapeDtypeStruct(roll_start.shape, jnp.float32),
            jax.ShapeDtypeStruct((rank, span), jnp.float32),
        ),
        in_specs=[pl.BlockSpec(memory_space=VMEM)] * 2,
        out_specs=[pl.BlockSpec(memory_space=VMEM)] * 2,
    )(roll_factor, mode_two)


def solution(mesh):
    in_specs = (P("roll", "mach", "cross"), P(None, "roll"), P(None, "mach"), P(None, "cross"))
    out_specs = (P(None, "roll"), P(None, ("mach", "cross")))
    return jax.shard_map(local, mesh=mesh, in_specs=in_specs, out_specs=out_specs, check_vma=False)
```
